512 devices in a mesh: seq: 64 (over z, y), head: 8 (over x, core).
Axes of the slice: x: 4, y: 4, z: 16, core: 2. Of those that a mesh axis runs over, the one named last changes fastest.
Arguments:
- queries: bfloat16 [24576, 3072], P('seq', 'head'), as said below
- keys: bfloat16 [24576, 3072], P('seq', 'head'), as said below
- values: bfloat16 [24576, 3072], P('seq', 'head'), may hold values from -6 to 6
- image_tiles: int32 [17], replicated, may hold values from 1 to 21, 192 in all
Outputs:
- attended: bfloat16 [24576, 3072], P(('seq', 'head'))
The draws below stay inside these ranges and needn't reach their ends.
Inputs may be any that keep to these rules, and one draw needn't show every extreme that they name: `image_tiles`: the 17 images fill all 192 tiles in order; the longest holds exactly 21 tiles. `queries`: entries lie within -6 and 6. `keys`: entries lie within -6 and 6.
All inputs are finite; a program needn't handle non-finite values.
Results may differ from the reference program's by a relative error of at most 0.007.
Values may be sent and summed in bfloat16 or wider, within the bound.
A program may use at most 64 MiB of HBM per device.

```python
import math
import jax
import jax.numpy as jnp
import numpy as np
from jax import lax

HEAD_DIM = 128
TILE = 128
HEADS = 24
WIDTH = 3072
TOKENS = 24576
NT = 192
MOST_TILES = 21
IMAGES = 17


def base_draw(key):
    return jnp.clip(jax.random.normal(key, (TOKENS, WIDTH), jnp.float32), -6.0, 6.0)


def draw_queries(key, part):
    drawn = base_draw(jax.random.fold_in(key, 21))
    return drawn.astype(jnp.bfloat16)


def draw_keys(key, part):
    drawn = base_draw(jax.random.fold_in(key, 22))
    return drawn.astype(jnp.bfloat16)


def block_scale(key, dims, pieces, low, high):
    loudness, own = 1.0, jax.random.fold_in(key, 6)
    for axis_at, shards_of in pieces:
        heights = jnp.exp(jax.random.uniform(jax.random.fold_in(own, axis_at), (shards_of,), jnp.float32, low / len(pieces), high / len(pieces)))
        loudness = loudness * jnp.repeat(heights, dims[axis_at] // shards_of).reshape([-1 if axis == axis_at else 1 for axis in range(len(dims))])
    return loudness


def length_profile(number_of, total, bound, lean):
    portions = [(1 << 20) // math.isqrt(grade ** lean) + 1 for grade in range(2, number_of + 1)]
    surplus, counts = total - bound - (number_of - 1), [1] * (number_of - 1)
    while surplus > 0:
        free = [i for i in range(number_of - 1) if counts[i] < bound]
        mass, remaining = sum([portions[i] for i in free]), surplus
        for i in free:
            more = min(bound - counts[i], max(1, remaining * portions[i] // mass), surplus)
            counts[i] = counts[i] + more
            surplus = surplus - more
    return np.array([bound] + counts)


def uneven_parts(own_key, amount, total, limit, lean):
    if amount == 2:
        one = jax.random.randint(own_key, (), max(1, total - limit), min(limit, total - 1) + 1)
        return jnp.stack([one, total - one])
    sizes = jnp.asarray(length_profile(amount, total, limit, lean), jnp.int32)
    couples = (amount - 1) // 2
    source_of, receiver = sizes[1:1 + 2 * couples:2], sizes[2:2 + 2 * couples:2]
    room = jnp.minimum(source_of - 1, limit - receiver)
    shifted = jax.random.randint(jax.random.fold_in(own_key, 1), (couples,), 0, 1 << 20) % (room + 1)
    sizes = sizes.at[1:1 + 2 * couples:2].set(source_of - shifted).at[2:2 + 2 * couples:2].set(receiver + shifted)
    return sizes[jax.random.permutation(jax.random.fold_in(own_key, 2), amount)]


def normal_values(stream_key, extent, width, most, split=(), kind=jnp.bfloat16):
    array = width * jax.random.normal(stream_key, extent, jnp.float32)
    if split:
        array = array * block_scale(stream_key, extent, split, -0.22, 0.18)
    return jnp.clip(array, -most, most).astype(kind)


def setup_inputs(seed: int = 0) -> dict:
    splits = jax.random.split(jax.random.key(seed), 5)
    queries = draw_queries(jax.random.fold_in(splits[4], 71), 0)
    keys = draw_keys(jax.random.fold_in(splits[4], 71), 0)
    values = normal_values(splits[2], (TOKENS, WIDTH), 1.0, 6.0, ((0, 64), (1, 8)))
    image_tiles = uneven_parts(splits[3], IMAGES, NT, MOST_TILES, 2).astype(jnp.int32)
    return dict(queries=queries, keys=keys, values=values, image_tiles=image_tiles)


def image_of(positions, image_tiles):
    image_ends = jnp.cumsum(image_tiles).astype(jnp.int32) * TILE
    return lax.optimization_barrier(jnp.sum((positions[:, None] >= image_ends[None, :]).astype(jnp.int32), axis=1)).astype(jnp.int32)

def reference(queries, keys, values, image_tiles):
    positions = jnp.arange(TOKENS, dtype=jnp.int32)
    token_image = image_of(positions, image_tiles)
    image_starts = (jnp.cumsum(image_tiles) - image_tiles).astype(jnp.int32) * TILE
    window = MOST_TILES * TILE
    padded_keys = jnp.pad(keys, ((0, window), (0, 0)))
    padded_values = jnp.pad(values, ((0, window), (0, 0)))
    padded_images = jnp.pad(token_image, (0, window), constant_values=-1)
    score_scale = 1.0 / math.sqrt(HEAD_DIM)

    def one_tile(tile_index):
        first_row = (tile_index * TILE).astype(jnp.int32)
        query_tile = lax.dynamic_slice_in_dim(queries, first_row, TILE, 0)
        image_index = token_image[first_row]
        key_start = image_starts[image_index].astype(jnp.int32)
        key_tile = lax.dynamic_slice_in_dim(padded_keys, key_start, window, 0)
        value_tile = lax.dynamic_slice_in_dim(padded_values, key_start, window, 0)
        key_images = lax.dynamic_slice_in_dim(padded_images, key_start, window, 0)
        query_heads = query_tile.reshape(TILE, HEADS, HEAD_DIM).astype(jnp.float32)
        key_heads = key_tile.reshape(window, HEADS, HEAD_DIM).astype(jnp.float32)
        value_heads = value_tile.reshape(window, HEADS, HEAD_DIM).astype(jnp.float32)
        scores = jnp.einsum('qhd,khd->hqk', query_heads, key_heads) * score_scale
        key_mask = (key_images == image_index)[None, None, :]
        scores = jnp.where(key_mask, scores, -jnp.inf)
        largest = lax.optimization_barrier(jnp.max(scores, axis=2, keepdims=True))
        weights = jnp.where(key_mask, jnp.exp(scores - largest), 0.0)
        weight_total = lax.optimization_barrier(jnp.sum(weights, axis=2))
        rounded = lax.optimization_barrier(weights.astype(jnp.bfloat16)).astype(jnp.float32)
        summed = jnp.einsum('hqk,khd->qhd', rounded, value_heads)
        attended = summed / jnp.transpose(weight_total)[:, :, None]
        return attended.reshape(TILE, WIDTH).astype(jnp.bfloat16)
    tiles = lax.map(one_tile, jnp.arange(TOKENS // TILE, dtype=jnp.int32))
    return tiles.reshape(TOKENS, WIDTH)
```

```python
import math

import jax
import jax.numpy as jnp
from jax import lax
from jax.experimental import pallas as pl
from jax.experimental.pallas import tpu as pltpu
from jax.sharding import PartitionSpec as P

MESH = pl.DeviceIdType.MESH
HD = 128
YS = 4
ZS = 16
HOMES = 3
ROWS = 384
PLANE = YS * ROWS
PLANE_TILES = PLANE // HD
NEG = -1e30


def gather_kernel(q_ref, k_ref, v_ref, qg, kw, vw, here_sem, near_send, near_recv, q_send, q_recv,
                  up_send, up_recv, down_send, down_recv):
    seq = lax.axis_index("seq")
    y = lax.rem(seq, YS)
    z = seq // YS
    base = z * YS
    above = lax.rem(z + 1, ZS) * YS + y
    below = lax.rem(z + ZS - 1, ZS) * YS + y

    barrier = pltpu.get_barrier_semaphore()
    for step in range(1, YS):
        pl.semaphore_signal(barrier, inc=1, device_id={"seq": base + lax.rem(y + step, YS)}, device_id_type=MESH)
    for other in (above, below):
        pl.semaphore_signal(barrier, inc=1, device_id={"seq": other}, device_id_type=MESH)
    pl.semaphore_wait(barrier, YS + 1)

    def remote(src, dst, send, recv, target):
        return pltpu.make_async_remote_copy(
            src_ref=src, dst_ref=dst, send_sem=send, recv_sem=recv,
            device_id={"seq": target}, device_id_type=MESH)

    pairs = ((k_ref, kw), (v_ref, vw))

    def near(j, n):
        src, win = pairs[n]
        return remote(src.at[:, pl.ds(j * HD, HD)], win.at[2, y], near_send.at[j, n], near_recv.at[y, n], base + j)

    def near_q(j):
        return remote(q_ref.at[:, pl.ds(j * HD, HD)], qg.at[y], q_send.at[j], q_recv.at[y], base + j)

    def own(n):
        src, win = ((k_ref, kw), (v_ref, vw), (q_ref, qg))[n]
        mine = pl.multiple_of(y * HD, HD)
        dst = win.at[2, y] if n < 2 else win.at[y]
        return pltpu.make_async_copy(src.at[:, pl.ds(mine, HD)], dst, here_sem.at[n])

    for j in range(HOMES):
        @pl.when(y != j)
        def _():
            near(j, 0).start()
            near(j, 1).start()

    home = y < HOMES

    @pl.when(home)
    def _():
        for n in range(3):
            own(n).start()

    for j in range(HOMES):
        @pl.when(y != j)
        def _():
            near_q(j).start()

    def part(win, p, yy, lo, hi):
        return win.at[p, yy, pl.ds(lo, hi - lo)]

    def first_up(yy, n):
        win = pairs[n][1]
        return remote(win.at[2, yy], win.at[1, yy], up_send.at[0, yy, n], up_recv.at[0, yy, n], above)

    def first_down(yy, n):
        win = pairs[n][1]
        return remote(win.at[2, yy], win.at[3, yy], down_send.at[0, yy, n], down_recv.at[0, yy, n], below)

    def second_up(yy, n):
        win = pairs[n][1]
        lo = HD if yy == 1 else 0
        return remote(part(win, 1, yy, lo, ROWS), part(win, 0, yy, lo, ROWS),
                      up_send.at[1, yy, n], up_recv.at[1, yy, n], above)

    def second_down(yy, n):
        win = pairs[n][1]
        hi = ROWS - HD if yy == 2 else ROWS
        return remote(part(win, 3, yy, 0, hi), part(win, 4, yy, 0, hi),
                      down_send.at[1, yy, n], down_recv.at[1, yy, n], below)

    @pl.when(home)
    def _():
        for n in range(2):
            own(n).wait()
            first_up(y, n).start()
            first_down(y, n).start()
        order = (2, 1, 3, 0)
        for yy in order:
            @pl.when(y != yy)
            def _():
                for n in range(2):
                    src, win = pairs[n]
                    remote(src.at[:, pl.ds(0, HD)], win.at[2, yy], near_send.at[0, n], near_recv.at[yy, n],
                           base).wait_recv()
                    first_up(yy, n).start()
                    first_down(yy, n).start()
        for up, down in ((2, 1), (1, 2), (3, 0)):
            for n in range(2):
                first_up(up, n).wait_recv()
                second_up(up, n).start()
                first_down(down, n).wait_recv()
                second_down(down, n).start()
        for n in range(2):
            first_up(0, n).wait_recv()
            first_down(3, n).wait_recv()
            for up, down in ((2, 1), (1, 2), (3, 0)):
                second_up(up, n).wait_recv()
                second_down(down, n).wait_recv()
        own(2).wait()
        for yy in range(YS):
            @pl.when(y != yy)
            def _():
                remote(q_ref.at[:, pl.ds(0, HD)], qg.at[yy], q_send.at[0], q_recv.at[yy], base).wait_recv()
        for n in range(2):
            for yy in range(YS):
                first_up(yy, n).wait_send()
                first_down(yy, n).wait_send()
            for up, down in ((2, 1), (1, 2), (3, 0)):
                second_up(up, n).wait_send()
                second_down(down, n).wait_send()

    for j in range(HOMES):
        @pl.when(y != j)
        def _():
            near(j, 0).wait_send()
            near(j, 1).wait_send()
            near_q(j).wait_send()


def gather(q, k, v):
    any_space = pl.BlockSpec(memory_space=pl.ANY)
    window = jax.ShapeDtypeStruct((5, YS, ROWS, HD), jnp.bfloat16)
    dma = pltpu.SemaphoreType.DMA
    return pl.pallas_call(
        gather_kernel,
        out_shape=(jax.ShapeDtypeStruct((YS, ROWS, HD), jnp.bfloat16), window, window),
        in_specs=[any_space] * 3,
        out_specs=(any_space,) * 3,
        scratch_shapes=[dma((3,)), dma((HOMES, 2)), dma((YS, 2)), dma((HOMES,)), dma((YS,)),
                        dma((2, YS, 2)), dma((2, YS, 2)), dma((2, YS, 2)), dma((2, YS, 2))],
        compiler_params=pltpu.CompilerParams(collective_id=0, has_side_effects=True),
        name="gather",
    )(q, k, v)


def attend_kernel(table, q_ref, k_ref, v_ref, o_ref, s_ref):
    scale = math.log2(math.e) / math.sqrt(HD)

    def job(first, rows, key_first, key_tiles):
        q = q_ref[pl.ds(pl.multiple_of(first * HD, HD), rows), :]
        chunks = (key_tiles + 1) // 2
        columns = lax.broadcasted_iota(jnp.int32, (rows, 2 * HD), 1)

        def chunk_at(i):
            return jnp.minimum(2 * i, jnp.maximum(key_tiles - 2, 0))

        def score(i, top):
            at = chunk_at(i)
            keys = k_ref[pl.ds(pl.multiple_of((key_first + at) * HD, HD), 2 * HD), :]
            s = lax.dot_general(q, keys, (((1,), (1,)), ((), ())), preferred_element_type=jnp.float32)
            fresh = (columns >= (2 * i - at) * HD) & (columns < (key_tiles - at) * HD)
            s = jnp.where(fresh, s, NEG)
            s_ref[i, :rows, :] = s
            return jnp.maximum(top, jnp.maximum(s[:, :HD], s[:, HD:]))

        top = lax.fori_loop(0, chunks, score, jnp.full((rows, HD), NEG, jnp.float32))
        m = jnp.max(top, axis=1, keepdims=True)

        def fold(i, carried):
            acc, total = carried
            p = jnp.exp2((s_ref[i, :rows, :] - m) * scale)
            start = pl.multiple_of((key_first + chunk_at(i)) * HD, HD)
            acc = acc + jnp.dot(p.astype(jnp.bfloat16), v_ref[pl.ds(start, 2 * HD), :],
                                preferred_element_type=jnp.float32)
            return acc, total + p[:, :HD] + p[:, HD:]

        zero = jnp.zeros((rows, HD), jnp.float32)
        acc, total = lax.fori_loop(0, chunks, fold, (zero, zero))
        o = acc / jnp.sum(total, axis=1, keepdims=True)
        o_ref[pl.ds(pl.multiple_of(first * HD, HD), rows), :] = o.astype(jnp.bfloat16)

    def body(first):
        key_first = table[1 + 3 * first]
        key_tiles = table[2 + 3 * first]
        left = table[3 + 3 * first]
        for tiles, fits in ((2, left >= 2), (1, left < 2)):
            @pl.when(fits)
            def _(tiles=tiles):
                job(first, tiles * HD, key_first, key_tiles)
        return first + jnp.minimum(left, 2)

    lax.while_loop(lambda first: first < table[0], body, jnp.int32(0))


def attend(table, q, k, v):
    return pl.pallas_call(
        attend_kernel,
        out_shape=jax.ShapeDtypeStruct((PLANE, HD), jnp.bfloat16),
        grid_spec=pltpu.PrefetchScalarGridSpec(
            num_scalar_prefetch=1, grid=(),
            in_specs=[pl.BlockSpec(memory_space=pltpu.VMEM)] * 3,
            out_specs=pl.BlockSpec(memory_space=pltpu.VMEM),
            scratch_shapes=[pltpu.VMEM((11, 2 * HD, 2 * HD), jnp.float32)]),
        compiler_params=pltpu.CompilerParams(vmem_limit_bytes=40 * 2**20),
        name="attend",
    )(table, q, k, v)


def spread_kernel(o_ref, out_ref, here_sem, send_sem, recv_sem):
    seq = lax.axis_index("seq")
    head = lax.axis_index("head")
    heads = lax.axis_size("head")
    y = lax.rem(seq, YS)
    base = seq - y
    rows = ROWS // heads
    peers = YS * heads
    me = y * heads + head

    def ids(t):
        return {"seq": base + t // heads, "head": lax.rem(t, heads)}

    barrier = pltpu.get_barrier_semaphore()

    def greet(i, c):
        pl.semaphore_signal(barrier, inc=1, device_id=ids(lax.rem(me + i, peers)), device_id_type=MESH)
        return c

    lax.fori_loop(1, peers, greet, 0)
    pl.semaphore_wait(barrier, peers - 1)

    def column(t):
        return pl.multiple_of((lax.rem(t, heads) * HOMES + t // heads) * HD, HD)

    def copy(i):
        t = lax.rem(me + i, peers)
        return pltpu.make_async_remote_copy(
            src_ref=o_ref.at[pl.ds(pl.multiple_of(t * rows, rows), rows)],
            dst_ref=out_ref.at[:, pl.ds(column(me), HD)],
            send_sem=send_sem.at[i], recv_sem=recv_sem.at[me],
            device_id=ids(t), device_id_type=MESH)

    def from_peer(t):
        return pltpu.make_async_remote_copy(
            src_ref=o_ref.at[pl.ds(0, rows)],
            dst_ref=out_ref.at[:, pl.ds(column(t), HD)],
            send_sem=send_sem.at[0], recv_sem=recv_sem.at[t],
            device_id=ids(lax.rem(me + 1, peers)), device_id_type=MESH)

    home = y < HOMES
    mine = pltpu.make_async_copy(
        o_ref.at[pl.ds(pl.multiple_of(me * rows, rows), rows)],
        out_ref.at[:, pl.ds(column(me), HD)], here_sem)

    @pl.when(home)
    def _():
        def start(i, c):
            copy(i).start()
            return c

        lax.fori_loop(1, peers, start, 0)
        mine.start()

    def wait(t, c):
        @pl.when(t != me)
        def _():
            from_peer(t).wait_recv()
        return c

    lax.fori_loop(0, HOMES * heads, wait, 0)

    @pl.when(home)
    def _():
        mine.wait()

        def finish(i, c):
            copy(i).wait_send()
            return c

        lax.fori_loop(1, peers, finish, 0)


def spread(o, heads):
    dma = pltpu.SemaphoreType.DMA
    return pl.pallas_call(
        spread_kernel,
        out_shape=jax.ShapeDtypeStruct((ROWS // heads, HOMES * heads * HD), jnp.bfloat16),
        in_specs=[pl.BlockSpec(memory_space=pltpu.VMEM)],
        out_specs=pl.BlockSpec(memory_space=pltpu.VMEM),
        scratch_shapes=[dma, dma((YS * heads,)), dma((YS * heads,))],
        compiler_params=pltpu.CompilerParams(collective_id=1, has_side_effects=True),
        name="spread",
    )(o)


def tile_table(image_tiles):
    seq = lax.axis_index("seq")
    z = seq // YS
    images = jnp.arange(image_tiles.shape[0])
    ends = jnp.sum(jnp.where(images[None, :] <= images[:, None], image_tiles[None, :], 0), axis=1)
    tiles = z * PLANE_TILES + jnp.arange(PLANE_TILES, dtype=jnp.int32)
    before = tiles[:, None] >= ends[None, :]
    first = jnp.max(jnp.where(before, ends[None, :], 0), axis=1)
    last = jnp.min(jnp.where(before, 2**30, ends[None, :]), axis=1)
    window = (z - 2) * PLANE_TILES
    left = jnp.minimum(last, (z + 1) * PLANE_TILES) - tiles
    rows = jnp.stack([first - window, last - first, left], axis=1).reshape(-1)
    count = jnp.where(lax.rem(seq, YS) < HOMES, PLANE_TILES, 0)
    return jnp.concatenate([count[None], rows]).astype(jnp.int32)


def shards(queries, keys, values, image_tiles):
    q, k, v = gather(queries, keys, values)
    table = tile_table(image_tiles)
    o = attend(table, q.reshape(PLANE, HD), k.reshape(5 * PLANE, HD), v.reshape(5 * PLANE, HD))
    return spread(o, lax.axis_size("head"))


def solution(mesh):
    placed = (P("seq", "head"), P("seq", "head"), P("seq", "head"), P())
    return jax.shard_map(
        shards, mesh=mesh, in_specs=placed, out_specs=P(("seq", "head"), None), check_vma=False
    )
```

```python
import functools
import math

import jax
import jax.numpy as jnp
from jax import lax
from jax.experimental import pallas as pl
from jax.experimental.pallas import tpu as pltpu
from jax.sharding import PartitionSpec as P

MESH = pl.DeviceIdType.MESH
HD = 128
YS = 4
ZS = 16
HOMES = 3
ROWS = 384
TILES = ROWS // HD
PLANE = YS * ROWS
PLANE_TILES = PLANE // HD
REACH = 2
WIDE = 2 * REACH + 1
MASKED = -1e30
LOWEST = -1e20
SCALE = math.log2(math.e) / math.sqrt(HD)


def kernel(heads, tiles_ref, q_ref, k_ref, v_ref, out_ref, win, raw, qraw, qv, relay, bias, acc, top, total, o_v,
           stage_sem, own_sem, near_send, near_recv, q_send, q_recv, up_send, up_recv, down_send, down_recv,
           raw_send, raw_recv, relay_send, here_sem, out_send, out_recv):
    seq = lax.axis_index("seq")
    head = lax.axis_index("head")
    y = lax.rem(seq, YS)
    z = lax.div(seq, YS)
    base = z * YS
    above = lax.rem(z + 1, ZS) * YS + y
    below = lax.rem(z + ZS - 1, ZS) * YS + y
    home = y < HOMES
    relays = y == HOMES
    peers = YS * heads
    me = y * heads + head

    def block(p, yy, lo=0, hi=ROWS):
        return win.at[p, :, pl.ds(pl.multiple_of(yy * ROWS + lo, HD), hi - lo)]

    def rows_of(yy):
        return pl.ds(pl.multiple_of(yy * ROWS, ROWS), ROWS)

    def stage(j, n):
        dst = qraw.at[j] if n == 2 else raw.at[j, n]
        return pltpu.make_async_copy((k_ref, v_ref, q_ref)[n].at[:, pl.ds(j * HD, HD)], dst, stage_sem.at[j, n])

    def own(n):
        mine = pl.ds(pl.multiple_of(y * HD, HD), HD)
        dst = qv.at[rows_of(y)] if n == 2 else win.at[REACH, n, rows_of(y)]
        return pltpu.make_async_copy((k_ref, v_ref, q_ref)[n].at[:, mine], dst, own_sem.at[n])

    @pl.when(home)
    def _():
        for n in range(3):
            own(n).start()

    for n in range(3):
        for j in range(HOMES):
            @pl.when(y != j)
            def _():
                stage(j, n).start()

    def ids(t):
        return {"seq": base + lax.div(t, heads), "head": lax.rem(t, heads)}

    barrier = pltpu.get_barrier_semaphore()

    def greet(i, c):
        pl.semaphore_signal(barrier, inc=1, device_id=ids(lax.rem(me + i, peers)), device_id_type=MESH)
        return c

    for other in (above, below):
        pl.semaphore_signal(barrier, inc=1, device_id={"seq": other}, device_id_type=MESH)
    lax.fori_loop(1, peers, greet, 0)

    first = (z - REACH) * PLANE_TILES
    keys_at = first + lax.div(lax.broadcasted_iota(jnp.int32, (1, WIDE * PLANE), 1), HD)
    query_at = z * PLANE_TILES + lax.broadcasted_iota(jnp.int32, (16, 1), 0)
    key_image = jnp.where(keys_at < 0, -1, 0)
    query_image = jnp.zeros((16, 1), jnp.int32)
    end = jnp.int32(0)
    for i in range(tiles_ref.shape[0]):
        end = end + tiles_ref[i]
        key_image = key_image + jnp.where(keys_at >= end, 1, 0)
        query_image = query_image + jnp.where(query_at >= end, 1, 0)
    bias[...] = jnp.where(key_image == query_image, 0.0, MASKED)

    @pl.when(home)
    def _():
        acc[...] = jnp.zeros_like(acc)
        total[...] = jnp.zeros_like(total)
        top[...] = jnp.full_like(top, LOWEST)

    pl.semaphore_wait(barrier, peers + 1)

    def remote(src, dst, send, recv, target):
        return pltpu.make_async_remote_copy(
            src_ref=src, dst_ref=dst, send_sem=send, recv_sem=recv,
            device_id={"seq": target}, device_id_type=MESH)

    def near(j):
        return remote(raw.at[j], block(REACH, y), near_send.at[j], near_recv.at[REACH, y], base + j)

    def near_q(j):
        return remote(qraw.at[j], qv.at[rows_of(y)], q_send.at[j], q_recv.at[y], base + j)

    def along(yy, hop, up, lo=0, hi=ROWS):
        src, dst = ((REACH + 1 - hop, REACH - hop) if up else (REACH - 1 + hop, REACH + hop))
        send, recv = (up_send, up_recv) if up else (down_send, down_recv)
        return remote(block(src, yy, lo, hi), block(dst, yy, lo, hi), send.at[hop - 1, yy], recv.at[hop - 1, yy],
                      above if up else below)

    def raw_along(j, up):
        n = 0 if up else 1
        return remote(raw.at[j], relay.at[n, j], raw_send.at[n, j], raw_recv.at[n, j], above if up else below)

    def relayed(j, up):
        n = 0 if up else 1
        p = REACH - 1 if up else REACH + 1
        return remote(relay.at[n, j], block(p, HOMES), relay_send.at[n, j], near_recv.at[p, HOMES], base + j)

    def send_near(j):
        for n in range(2):
            stage(j, n).wait()
        near(j).start()

    def send_q(j):
        stage(j, 2).wait()
        near_q(j).start()

    def second(yy, up, act):
        if up:
            @pl.when(yy == 1)
            def _():
                act(along(yy, 2, True, HD, ROWS))

            @pl.when(yy > 1)
            def _():
                act(along(yy, 2, True))
        else:
            @pl.when(yy == 2)
            def _():
                act(along(yy, 2, False, 0, ROWS - HD))

            @pl.when(yy < 2)
            def _():
                act(along(yy, 2, False))

    begin = lambda copy: copy.start()
    arrived = lambda copy: copy.wait_recv()
    left = lambda copy: copy.wait_send()

    def fold(p, yy, tile_lo, tile_hi, row_lo, row_hi):
        count = tile_hi - tile_lo
        rows = pl.ds(row_lo, row_hi - row_lo)
        at = pl.multiple_of(yy * ROWS + tile_lo * HD, HD)
        keys = win[p, 0, pl.ds(at, count * HD), :]
        vals = win[p, 1, pl.ds(at, count * HD), :]
        lanes = pl.ds(pl.multiple_of(p * PLANE + yy * ROWS + tile_lo * HD, HD), count * HD)
        s = lax.dot_general(qv[rows, :], keys, (((1,), (1,)), ((), ())), preferred_element_type=jnp.float32)
        s = jnp.concatenate(
            [s[i:i + HD] * SCALE + bias[pl.ds((row_lo + i) // HD, 1), lanes] for i in range(0, row_hi - row_lo, HD)],
            axis=0)
        parts = [s[:, i * HD:(i + 1) * HD] for i in range(count)]
        old = top[rows, :]
        new = jnp.maximum(old, jnp.max(functools.reduce(jnp.maximum, parts), axis=1, keepdims=True))
        factor = jnp.exp2(old - new)
        weights = [jnp.exp2(part - new) for part in parts]
        total[rows, :] = total[rows, :] * factor + functools.reduce(jnp.add, weights)
        rounded = jnp.concatenate([w.astype(jnp.bfloat16) for w in weights], axis=1)
        acc[rows, :] = acc[rows, :] * factor + jnp.dot(rounded, vals, preferred_element_type=jnp.float32)
        top[rows, :] = new

    def whole(p, yy):
        fold(p, yy, 0, TILES, 0, PLANE)

    def column(t):
        return pl.ds(pl.multiple_of((lax.rem(t, heads) * HOMES + lax.div(t, heads)) * HD, HD), HD)

    out_rows = ROWS // heads

    def out_copy(t):
        return pltpu.make_async_remote_copy(
            src_ref=o_v.at[pl.ds(pl.multiple_of(t * out_rows, out_rows), out_rows)], dst_ref=out_ref.at[:, column(me)],
            send_sem=out_send.at[t], recv_sem=out_recv.at[me], device_id=ids(t), device_id_type=MESH)

    def out_here():
        return pltpu.make_async_copy(
            o_v.at[pl.ds(pl.multiple_of(me * out_rows, out_rows), out_rows)], out_ref.at[:, column(me)], here_sem)

    @pl.when(home)
    def _():
        a = jnp.where(y == 1, 0, 1)
        b = jnp.where(y == 2, 0, 2)
        own(0).wait()
        own(1).wait()
        for up in (True, False):
            along(y, 1, up).start()
        for j in (1, 0, 2):
            @pl.when(y != j)
            def _():
                send_near(j)
        for j in (1, 0, 2):
            @pl.when(y != j)
            def _():
                send_q(j)

        def near_arrived(yy):
            remote(raw.at[0], block(REACH, yy), near_send.at[0], near_recv.at[REACH, yy], base).wait_recv()

        def pass_on(yy):
            for up in (True, False):
                along(yy, 1, up).wait_recv()
                second(yy, up, begin)

        def relay_arrived(p):
            remote(raw.at[0], block(p, HOMES), near_send.at[0], near_recv.at[p, HOMES], base).wait_recv()

        near_arrived(a)
        for up in (True, False):
            along(a, 1, up).start()
        pass_on(y)
        near_arrived(b)
        for up in (True, False):
            along(b, 1, up).start()
        pass_on(a)
        own(2).wait()
        for yy in range(YS):
            @pl.when(y != yy)
            def _():
                remote(qraw.at[0], qv.at[rows_of(yy)], q_send.at[0], q_recv.at[yy], base).wait_recv()
        whole(REACH, y)
        pass_on(b)
        whole(REACH, a)
        whole(REACH, b)
        near_arrived(HOMES)
        relay_arrived(REACH - 1)
        second(HOMES, True, begin)
        whole(REACH, HOMES)
        for yy in (y, a, b):
            whole(REACH - 1, yy)
            whole(REACH + 1, yy)
        whole(REACH - 1, HOMES)
        relay_arrived(REACH + 1)
        whole(REACH + 1, HOMES)
        second(1, True, arrived)
        fold(0, 1, 1, 3, 0, ROWS)
        second(0, False, arrived)
        fold(4, 0, 0, 3, ROWS, PLANE)
        second(2, True, arrived)
        fold(0, 2, 0, 3, 0, 2 * ROWS)
        second(1, False, arrived)
        fold(4, 1, 0, 3, 2 * ROWS, PLANE)
        second(2, False, arrived)
        fold(4, 2, 0, 2, 3 * ROWS, PLANE)
        second(3, True, arrived)
        fold(0, 3, 0, 3, 0, 3 * ROWS)

        for yy in range(YS):
            rows = pl.ds(yy * ROWS, ROWS)
            o_v[rows, :] = (acc[rows, :] / jnp.sum(total[rows, :], axis=1, keepdims=True)).astype(jnp.bfloat16)

            def put(i, c):
                t = yy * heads + i

                @pl.when(t != me)
                def _():
                    out_copy(t).start()

                @pl.when(t == me)
                def _():
                    out_here().start()
                return c

            lax.fori_loop(0, heads, put, 0)

    @pl.when(relays)
    def _():
        order = (0, 2, 1)
        for j in order:
            for n in range(2):
                stage(j, n).wait()
            for up in (True, False):
                raw_along(j, up).start()
            near(j).start()
        for j in order:
            send_q(j)
        for j in order:
            for up in (True, False):
                raw_along(j, up).wait_recv()
                relayed(j, up).start()
        for j in order:
            for up in (True, False):
                raw_along(j, up).wait_send()
                relayed(j, up).wait_send()

    def out_wait(t, c):
        @pl.when(t != me)
        def _():
            pltpu.make_async_remote_copy(
                src_ref=o_v.at[pl.ds(0, out_rows)], dst_ref=out_ref.at[:, column(t)], send_sem=out_send.at[0],
                recv_sem=out_recv.at[t], device_id=ids(t), device_id_type=MESH).wait_recv()
        return c

    lax.fori_loop(0, HOMES * heads, out_wait, 0)

    @pl.when(home)
    def _():
        out_here().wait()

        def out_left(i, c):
            out_copy(lax.rem(me + i, peers)).wait_send()
            return c

        lax.fori_loop(1, peers, out_left, 0)
        for yy in range(HOMES):
            for up in (True, False):
                along(yy, 1, up).wait_send()
        for yy in range(1, YS):
            second(yy, True, left)
        for yy in range(HOMES):
            second(yy, False, left)

    for j in range(HOMES):
        @pl.when(y != j)
        def _():
            near(j).wait_send()
            near_q(j).wait_send()


def shards(queries, keys, values, image_tiles):
    heads = lax.axis_size("head")
    dma = pltpu.SemaphoreType.DMA
    half, whole = jnp.bfloat16, jnp.float32
    vmem = pltpu.VMEM
    any_space = pl.BlockSpec(memory_space=pl.ANY)
    return pl.pallas_call(
        functools.partial(kernel, heads),
        out_shape=jax.ShapeDtypeStruct((ROWS // heads, HOMES * heads * HD), half),
        in_specs=[pl.BlockSpec(memory_space=pltpu.SMEM), any_space, any_space, any_space],
        out_specs=pl.BlockSpec(memory_space=vmem),
        scratch_shapes=[
            vmem((WIDE, 2, PLANE, HD), half), vmem((HOMES, 2, ROWS, HD), half), vmem((HOMES, ROWS, HD), half),
            vmem((PLANE, HD), half), vmem((2, HOMES, 2, ROWS, HD), half), vmem((16, WIDE * PLANE), whole),
            vmem((PLANE, HD), whole), vmem((PLANE, HD), whole), vmem((PLANE, HD), whole), vmem((PLANE, HD), half),
            dma((HOMES, 3)), dma((3,)), dma((HOMES,)), dma((WIDE, YS)), dma((HOMES,)), dma((YS,)),
            dma((2, YS)), dma((2, YS)), dma((2, YS)), dma((2, YS)),
            dma((2, HOMES)), dma((2, HOMES)), dma((2, HOMES)), dma, dma((YS * heads,)), dma((YS * heads,))],
        compiler_params=pltpu.CompilerParams(
            collective_id=0, has_side_effects=True, vmem_limit_bytes=40 * 2**20),
        name="attend",
    )(image_tiles, queries, keys, values)


def solution(mesh):
    placed = (P("seq", "head"), P("seq", "head"), P("seq", "head"), P())
    return jax.shard_map(
        shards, mesh=mesh, in_specs=placed, out_specs=P(("seq", "head"), None), check_vma=False
    )
```

```python
import functools
import math

import jax
import jax.numpy as jnp
from jax import lax
from jax.experimental import pallas as pl
from jax.experimental.pallas import tpu as pltpu
from jax.sharding import PartitionSpec as P

MESH = pl.DeviceIdType.MESH
HD = 128
YS = 4
ZS = 16
HOMES = 3
ROWS = 384
TILES = ROWS // HD
PLANE = YS * ROWS
PLANE_TILES = PLANE // HD
REACH = 2
WIDE = 2 * REACH + 1
MASKED = -1e30
LOWEST = -1e20
SCALE = math.log2(math.e) / math.sqrt(HD)


def kernel(heads, tiles_hbm, q_ref, k_ref, v_ref, out_ref, win, raw, qraw, qv, relay, bias, acc, top, total, o_v,
           tiles_ref, stage_sem, own_sem, near_send, near_recv, q_send, q_recv, up_send, up_recv, down_send, down_recv,
           relay_sems, tiles_sem, here_sem, out_send, out_recv):
    seq = lax.axis_index("seq")
    head = lax.axis_index("head")
    y = lax.rem(seq, YS)
    z = lax.div(seq, YS)
    base = z * YS
    above = lax.rem(z + 1, ZS) * YS + y
    below = lax.rem(z + ZS - 1, ZS) * YS + y
    home = y < HOMES
    relays = y == HOMES
    peers = YS * heads
    me = y * heads + head

    def block(p, yy, lo=0, hi=ROWS):
        return win.at[p, :, pl.ds(pl.multiple_of(yy * ROWS + lo, HD), hi - lo)]

    def rows_of(yy):
        return pl.ds(pl.multiple_of(yy * ROWS, ROWS), ROWS)

    def stage(j, n):
        dst = qraw.at[j] if n == 2 else raw.at[j, n]
        return pltpu.make_async_copy((k_ref, v_ref, q_ref)[n].at[:, pl.ds(j * HD, HD)], dst, stage_sem.at[j, n])

    def own(n):
        mine = pl.ds(pl.multiple_of(y * HD, HD), HD)
        dst = qv.at[rows_of(y)] if n == 2 else win.at[REACH, n, rows_of(y)]
        return pltpu.make_async_copy((k_ref, v_ref, q_ref)[n].at[:, mine], dst, own_sem.at[n])

    fetch = pltpu.make_async_copy(tiles_hbm, tiles_ref, tiles_sem)
    fetch.start()

    @pl.when(home)
    def _():
        for n in range(3):
            own(n).start()

    for n in range(3):
        for j in range(HOMES):
            @pl.when(y != j)
            def _():
                stage(j, n).start()

    def ids(t):
        return {"seq": base + lax.div(t, heads), "head": lax.rem(t, heads)}

    barrier = pltpu.get_barrier_semaphore()

    def greet(i, c):
        pl.semaphore_signal(barrier, inc=1, device_id=ids(lax.rem(me + i, peers)), device_id_type=MESH)
        return c

    for other in (above, below):
        pl.semaphore_signal(barrier, inc=1, device_id={"seq": other}, device_id_type=MESH)
    lax.fori_loop(1, peers, greet, 0)

    first = (z - REACH) * PLANE_TILES
    keys_at = first + lax.div(lax.broadcasted_iota(jnp.int32, (1, WIDE * PLANE), 1), HD)
    query_at = z * PLANE_TILES + lax.broadcasted_iota(jnp.int32, (16, 1), 0)
    key_image = jnp.where(keys_at < 0, -1, 0)
    query_image = jnp.zeros((16, 1), jnp.int32)
    end = jnp.int32(0)
    fetch.wait()
    for i in range(tiles_ref.shape[0]):
        end = end + tiles_ref[i]
        key_image = key_image + jnp.where(keys_at >= end, 1, 0)
        query_image = query_image + jnp.where(query_at >= end, 1, 0)
    bias[...] = jnp.where(key_image == query_image, 0.0, MASKED)

    @pl.when(home)
    def _():
        acc[...] = jnp.zeros_like(acc)
        total[...] = jnp.zeros_like(total)
        top[...] = jnp.full_like(top, LOWEST)

    pl.semaphore_wait(barrier, peers + 1)

    def remote(src, dst, send, recv, target):
        return pltpu.make_async_remote_copy(
            src_ref=src, dst_ref=dst, send_sem=send, recv_sem=recv,
            device_id={"seq": target}, device_id_type=MESH)

    def near(j):
        return remote(raw.at[j], block(REACH, y), near_send.at[j], near_recv.at[REACH, y], base + j)

    def near_q(j):
        return remote(qraw.at[j], qv.at[rows_of(y)], q_send.at[j], q_recv.at[y], base + j)

    def along(yy, hop, up, lo=0, hi=ROWS):
        src, dst = ((REACH + 1 - hop, REACH - hop) if up else (REACH - 1 + hop, REACH + hop))
        send, recv = (up_send, up_recv) if up else (down_send, down_recv)
        return remote(block(src, yy, lo, hi), block(dst, yy, lo, hi), send.at[hop - 1, yy], recv.at[hop - 1, yy],
                      above if up else below)

    def relay_in():
        return remote(raw.at[1], relay, relay_sems.at[0], relay_sems.at[1], base + 2)

    def relay_out():
        return remote(relay, block(REACH, HOMES), relay_sems.at[2], near_recv.at[REACH, HOMES], base + 1)

    def sends(up):
        return z < ZS - 1 if up else z > 0

    def gets(up, hop=1):
        return z >= hop if up else z < ZS - hop

    def send_near(j):
        for n in range(2):
            stage(j, n).wait()
        near(j).start()

    def send_q(j):
        stage(j, 2).wait()
        near_q(j).start()

    def second(yy, up, act, where):
        short, first_short = (1, HD) if up else (2, 0)

        @pl.when(where & (yy == short))
        def _():
            act(along(yy, 2, up, first_short, first_short + ROWS - HD))

        @pl.when(where & ((yy > short) if up else (yy < short)))
        def _():
            act(along(yy, 2, up))

    begin = lambda copy: copy.start()
    arrived = lambda copy: copy.wait_recv()
    left = lambda copy: copy.wait_send()

    def fold(p, yy, tile_lo, tile_hi, row_lo, row_hi):
        count = tile_hi - tile_lo
        rows = pl.ds(row_lo, row_hi - row_lo)
        at = pl.multiple_of(yy * ROWS + tile_lo * HD, HD)
        keys = win[p, 0, pl.ds(at, count * HD), :]
        vals = win[p, 1, pl.ds(at, count * HD), :]
        lanes = pl.ds(pl.multiple_of(p * PLANE + yy * ROWS + tile_lo * HD, HD), count * HD)
        s = lax.dot_general(qv[rows, :], keys, (((1,), (1,)), ((), ())), preferred_element_type=jnp.float32)
        s = jnp.concatenate(
            [s[i:i + HD] * SCALE + bias[pl.ds((row_lo + i) // HD, 1), lanes] for i in range(0, row_hi - row_lo, HD)],
            axis=0)
        parts = [s[:, i * HD:(i + 1) * HD] for i in range(count)]
        old = top[rows, :]
        new = jnp.maximum(old, jnp.max(functools.reduce(jnp.maximum, parts), axis=1, keepdims=True))
        factor = jnp.exp2(old - new)
        weights = [jnp.exp2(part - new) for part in parts]
        total[rows, :] = total[rows, :] * factor + functools.reduce(jnp.add, weights)
        rounded = jnp.concatenate([w.astype(jnp.bfloat16) for w in weights], axis=1)
        acc[rows, :] = acc[rows, :] * factor + jnp.dot(rounded, vals, preferred_element_type=jnp.float32)
        top[rows, :] = new

    def whole(p, yy):
        fold(p, yy, 0, TILES, 0, PLANE)

    def column(t):
        return pl.ds(pl.multiple_of((lax.rem(t, heads) * HOMES + lax.div(t, heads)) * HD, HD), HD)

    out_rows = ROWS // heads

    def out_copy(t):
        return pltpu.make_async_remote_copy(
            src_ref=o_v.at[pl.ds(pl.multiple_of(t * out_rows, out_rows), out_rows)], dst_ref=out_ref.at[:, column(me)],
            send_sem=out_send.at[t], recv_sem=out_recv.at[me], device_id=ids(t), device_id_type=MESH)

    def out_here():
        return pltpu.make_async_copy(
            o_v.at[pl.ds(pl.multiple_of(me * out_rows, out_rows), out_rows)], out_ref.at[:, column(me)], here_sem)

    @pl.when(home)
    def _():
        a = jnp.where(y == 1, 0, 1)
        b = jnp.where(y == 2, 0, 2)

        def start_along(yy):
            for up in (True, False):
                @pl.when(sends(up))
                def _():
                    along(yy, 1, up).start()

        def near_arrived(yy):
            remote(raw.at[0], block(REACH, yy), near_send.at[0], near_recv.at[REACH, yy], base).wait_recv()

        def pass_on(yy):
            for up in (True, False):
                @pl.when(gets(up))
                def _():
                    along(yy, 1, up).wait_recv()
                second(yy, up, begin, gets(up) & sends(up))

        def fold_along(yy):
            for up in (True, False):
                @pl.when(gets(up))
                def _():
                    whole(REACH - 1 if up else REACH + 1, yy)

        def far(yy, up, tile_lo, tile_hi, row_lo, row_hi):
            second(yy, up, arrived, gets(up, 2))

            @pl.when(gets(up, 2))
            def _():
                fold(0 if up else 4, yy, tile_lo, tile_hi, row_lo, row_hi)

        own(0).wait()
        own(1).wait()
        start_along(y)

        @pl.when(y == 0)
        def _():
            send_near(1)
            near(1).wait_send()
            send_near(2)

        @pl.when(y == 1)
        def _():
            send_near(0)
            send_near(2)

        @pl.when(y == 2)
        def _():
            send_near(1)
            send_near(0)
            relay_in().wait_recv()
            relay_out().start()

        near_arrived(a)
        start_along(a)
        for j in (1, 0, 2):
            @pl.when(y != j)
            def _():
                send_q(j)
        pass_on(y)
        near_arrived(b)
        start_along(b)
        near_arrived(HOMES)
        start_along(HOMES)
        pass_on(a)
        own(2).wait()
        for yy in range(YS):
            @pl.when(y != yy)
            def _():
                remote(qraw.at[0], qv.at[rows_of(yy)], q_send.at[0], q_recv.at[yy], base).wait_recv()
        whole(REACH, y)
        whole(REACH, a)
        whole(REACH, b)
        pass_on(b)
        whole(REACH, HOMES)
        fold_along(y)
        fold_along(a)
        pass_on(HOMES)
        fold_along(b)
        fold_along(HOMES)
        far(1, True, 1, 3, 0, ROWS)
        far(0, False, 0, 3, ROWS, PLANE)
        far(2, True, 0, 3, 0, 2 * ROWS)
        far(1, False, 0, 3, 2 * ROWS, PLANE)
        far(2, False, 0, 2, 3 * ROWS, PLANE)
        far(3, True, 0, 3, 0, 3 * ROWS)

        for yy in range(YS):
            rows = pl.ds(yy * ROWS, ROWS)
            o_v[rows, :] = (acc[rows, :] / jnp.sum(total[rows, :], axis=1, keepdims=True)).astype(jnp.bfloat16)

            def put(i, c):
                t = yy * heads + i

                @pl.when(t != me)
                def _():
                    out_copy(t).start()

                @pl.when(t == me)
                def _():
                    out_here().start()
                return c

            lax.fori_loop(0, heads, put, 0)

    @pl.when(relays)
    def _():
        for n in range(2):
            stage(1, n).wait()
        relay_in().start()
        send_near(0)
        relay_in().wait_send()
        send_near(2)
        for j in (0, 2, 1):
            send_q(j)

    def out_wait(t, c):
        @pl.when(t != me)
        def _():
            pltpu.make_async_remote_copy(
                src_ref=o_v.at[pl.ds(0, out_rows)], dst_ref=out_ref.at[:, column(t)], send_sem=out_send.at[0],
                recv_sem=out_recv.at[t], device_id=ids(t), device_id_type=MESH).wait_recv()
        return c

    lax.fori_loop(0, HOMES * heads, out_wait, 0)

    @pl.when(home)
    def _():
        out_here().wait()

        def out_left(i, c):
            out_copy(lax.rem(me + i, peers)).wait_send()
            return c

        lax.fori_loop(1, peers, out_left, 0)
        for up in (True, False):
            for yy in range(YS):
                @pl.when(sends(up))
                def _():
                    along(yy, 1, up).wait_send()
                if (yy > 0) if up else (yy < HOMES):
                    second(yy, up, left, gets(up) & sends(up))

        @pl.when(y == 2)
        def _():
            relay_out().wait_send()

    for j in range(HOMES):
        sent = y != j
        direct = sent & (y != HOMES) if j == 1 else sent

        @pl.when(direct & ((y != 0) | (j != 1)))
        def _():
            near(j).wait_send()

        @pl.when(sent)
        def _():
            near_q(j).wait_send()


def shards(queries, keys, values, image_tiles):
    heads = lax.axis_size("head")
    dma = pltpu.SemaphoreType.DMA
    half, whole = jnp.bfloat16, jnp.float32
    vmem = pltpu.VMEM
    return pl.pallas_call(
        functools.partial(kernel, heads),
        out_shape=jax.ShapeDtypeStruct((ROWS // heads, HOMES * heads * HD), half),
        in_specs=[pl.BlockSpec(memory_space=pltpu.HBM)] * 4,
        out_specs=pl.BlockSpec(memory_space=vmem),
        scratch_shapes=[
            vmem((WIDE, 2, PLANE, HD), half), vmem((HOMES, 2, ROWS, HD), half), vmem((HOMES, ROWS, HD), half),
            vmem((PLANE, HD), half), vmem((2, ROWS, HD), half), vmem((16, WIDE * PLANE), whole),
            vmem((PLANE, HD), whole), vmem((PLANE, HD), whole), vmem((PLANE, HD), whole), vmem((PLANE, HD), half),
            pltpu.SMEM(image_tiles.shape, jnp.int32), dma((HOMES, 3)), dma((3,)), dma((HOMES,)), dma((WIDE, YS)), dma((HOMES,)), dma((YS,)),
            dma((2, YS)), dma((2, YS)), dma((2, YS)), dma((2, YS)),
            dma((3,)), dma, dma, dma((YS * heads,)), dma((YS * heads,))],
        compiler_params=pltpu.CompilerParams(
            collective_id=0, has_side_effects=True, vmem_limit_bytes=64 * 2**20),
        name="attend",
    )(image_tiles, queries, keys, values)


def solution(mesh):
    placed = (P("seq", "head"), P("seq", "head"), P("seq", "head"), P())
    return jax.shard_map(
        shards, mesh=mesh, in_specs=placed, out_specs=P(("seq", "head"), None), check_vma=False
    )
```

```python
import functools
import math

import jax
import jax.numpy as jnp
from jax import lax
from jax.experimental import pallas as pl
from jax.experimental.pallas import tpu as pltpu
from jax.sharding import PartitionSpec as P

MESH = pl.DeviceIdType.MESH
HD = 128
YS = 4
ZS = 16
HOMES = 3
ROWS = 384
TILES = ROWS // HD
PLANE = YS * ROWS
PLANE_TILES = PLANE // HD
REACH = 2
CARRIED = 2 * HD
WIDE = 2 * REACH + 1
MASKED = -1e30
LOWEST = -1e20
SCALE = math.log2(math.e) / math.sqrt(HD)


def kernel(heads, tiles_hbm, q_ref, k_ref, v_ref, out_ref, win, raw, qraw, qv, relay, bias, acc, top, total, o_v,
           carried, tiles_ref, stage_sem, own_sem, near_send, near_recv, q_send, q_recv, up_send, up_recv, down_send, down_recv,
           relay_sems, carry_send, carry_recv, hand_send, tiles_sem, here_sem, out_send, out_recv):
    seq = lax.axis_index("seq")
    head = lax.axis_index("head")
    y = lax.rem(seq, YS)
    z = lax.div(seq, YS)
    base = z * YS
    above = lax.rem(z + 1, ZS) * YS + y
    below = lax.rem(z + ZS - 1, ZS) * YS + y
    home = y < HOMES
    relays = y == HOMES
    peers = YS * heads
    me = y * heads + head

    def block(p, yy, lo=0, hi=ROWS):
        return win.at[p, :, pl.ds(pl.multiple_of(yy * ROWS + lo, HD), hi - lo)]

    def rows_of(yy):
        return pl.ds(pl.multiple_of(yy * ROWS, ROWS), ROWS)

    def stage(j, n):
        dst = qraw.at[j] if n == 2 else raw.at[j, n]
        return pltpu.make_async_copy((k_ref, v_ref, q_ref)[n].at[:, pl.ds(j * HD, HD)], dst, stage_sem.at[j, n])

    def own(n):
        mine = pl.ds(pl.multiple_of(y * HD, HD), HD)
        dst = qv.at[rows_of(y)] if n == 2 else win.at[REACH, n, rows_of(y)]
        return pltpu.make_async_copy((k_ref, v_ref, q_ref)[n].at[:, mine], dst, own_sem.at[n])

    fetch = pltpu.make_async_copy(tiles_hbm, tiles_ref, tiles_sem)
    fetch.start()

    @pl.when(home)
    def _():
        for n in range(3):
            own(n).start()

    for n in range(3):
        for j in range(HOMES):
            @pl.when(y != j)
            def _():
                stage(j, n).start()

    def ids(t):
        return {"seq": base + lax.div(t, heads), "head": lax.rem(t, heads)}

    barrier = pltpu.get_barrier_semaphore()

    def greet(i, c):
        pl.semaphore_signal(barrier, inc=1, device_id=ids(lax.rem(me + i, peers)), device_id_type=MESH)
        return c

    for other in (above, below):
        pl.semaphore_signal(barrier, inc=1, device_id={"seq": other}, device_id_type=MESH)
    lax.fori_loop(1, peers, greet, 0)

    first = (z - REACH) * PLANE_TILES
    keys_at = first + lax.div(lax.broadcasted_iota(jnp.int32, (1, WIDE * PLANE), 1), HD)
    query_at = z * PLANE_TILES + lax.broadcasted_iota(jnp.int32, (16, 1), 0)
    key_image = jnp.where(keys_at < 0, -1, 0)
    query_image = jnp.zeros((16, 1), jnp.int32)
    end = jnp.int32(0)
    fetch.wait()
    for i in range(tiles_ref.shape[0]):
        end = end + tiles_ref[i]
        key_image = key_image + jnp.where(keys_at >= end, 1, 0)
        query_image = query_image + jnp.where(query_at >= end, 1, 0)
    bias[...] = jnp.where(key_image == query_image, 0.0, MASKED)

    @pl.when(home)
    def _():
        acc[...] = jnp.zeros_like(acc)
        total[...] = jnp.zeros_like(total)
        top[...] = jnp.full_like(top, LOWEST)

    pl.semaphore_wait(barrier, peers + 1)

    def remote(src, dst, send, recv, target):
        return pltpu.make_async_remote_copy(
            src_ref=src, dst_ref=dst, send_sem=send, recv_sem=recv,
            device_id={"seq": target}, device_id_type=MESH)

    def near(j):
        return remote(raw.at[j], block(REACH, y), near_send.at[j], near_recv.at[REACH, y], base + j)

    def near_q(j):
        return remote(qraw.at[j], qv.at[rows_of(y)], q_send.at[j], q_recv.at[y], base + j)

    def along(yy, hop, up, lo=0, hi=ROWS):
        src, dst = ((REACH + 1 - hop, REACH - hop) if up else (REACH - 1 + hop, REACH + hop))
        send, recv = (up_send, up_recv) if up else (down_send, down_recv)
        return remote(block(src, yy, lo, hi), block(dst, yy, lo, hi), send.at[hop - 1, yy], recv.at[hop - 1, yy],
                      above if up else below)

    def relay_in():
        return remote(raw.at[1], relay, relay_sems.at[0], relay_sems.at[1], base + 2)

    def relay_out():
        return remote(relay, block(REACH, HOMES), relay_sems.at[2], near_recv.at[REACH, HOMES], base + 1)

    def carry(j, up):
        n = 0 if up else 1
        return remote(raw.at[j, :, pl.ds(ROWS - CARRIED, CARRIED)], carried.at[n, j], carry_send.at[n, j],
                      carry_recv.at[n, j], above if up else below)

    def hand(j, up):
        n, p = (0, REACH - 1) if up else (1, REACH + 1)
        return remote(carried.at[n, j], block(p, HOMES, ROWS - CARRIED, ROWS), hand_send.at[n, j],
                      near_recv.at[p, HOMES], base + j)

    def sends(up):
        return z < ZS - 1 if up else z > 0

    def gets(up, hop=1):
        return z >= hop if up else z < ZS - hop

    def send_near(j):
        for n in range(2):
            stage(j, n).wait()
        near(j).start()

    def send_q(j):
        stage(j, 2).wait()
        near_q(j).start()

    def second(yy, up, act, where):
        short, first_short = (1, HD) if up else (2, 0)

        @pl.when(where & (yy == short))
        def _():
            act(along(yy, 2, up, first_short, first_short + ROWS - HD))

        @pl.when(where & ((yy > short) if up else (yy < short)))
        def _():
            act(along(yy, 2, up))

    def first_hop(yy, up, act, where):
        @pl.when(where & (yy == HOMES))
        def _():
            act(along(yy, 1, up, 0, ROWS - CARRIED))

        @pl.when(where & (yy != HOMES))
        def _():
            act(along(yy, 1, up))

    begin = lambda copy: copy.start()
    arrived = lambda copy: copy.wait_recv()
    left = lambda copy: copy.wait_send()

    def fold(p, yy, tile_lo, tile_hi, row_lo, row_hi):
        count = tile_hi - tile_lo
        rows = pl.ds(row_lo, row_hi - row_lo)
        at = pl.multiple_of(yy * ROWS + tile_lo * HD, HD)
        keys = win[p, 0, pl.ds(at, count * HD), :]
        vals = win[p, 1, pl.ds(at, count * HD), :]
        lanes = pl.ds(pl.multiple_of(p * PLANE + yy * ROWS + tile_lo * HD, HD), count * HD)
        s = lax.dot_general(qv[rows, :], keys, (((1,), (1,)), ((), ())), preferred_element_type=jnp.float32)
        s = jnp.concatenate(
            [s[i:i + HD] * SCALE + bias[pl.ds((row_lo + i) // HD, 1), lanes] for i in range(0, row_hi - row_lo, HD)],
            axis=0)
        parts = [s[:, i * HD:(i + 1) * HD] for i in range(count)]
        old = top[rows, :]
        new = jnp.maximum(old, jnp.max(functools.reduce(jnp.maximum, parts), axis=1, keepdims=True))
        factor = jnp.exp2(old - new)
        weights = [jnp.exp2(part - new) for part in parts]
        total[rows, :] = total[rows, :] * factor + functools.reduce(jnp.add, weights)
        rounded = jnp.concatenate([w.astype(jnp.bfloat16) for w in weights], axis=1)
        acc[rows, :] = acc[rows, :] * factor + jnp.dot(rounded, vals, preferred_element_type=jnp.float32)
        top[rows, :] = new

    def whole(p, yy):
        fold(p, yy, 0, TILES, 0, PLANE)

    def column(t):
        return pl.ds(pl.multiple_of((lax.rem(t, heads) * HOMES + lax.div(t, heads)) * HD, HD), HD)

    out_rows = ROWS // heads

    def out_copy(t):
        return pltpu.make_async_remote_copy(
            src_ref=o_v.at[pl.ds(pl.multiple_of(t * out_rows, out_rows), out_rows)], dst_ref=out_ref.at[:, column(me)],
            send_sem=out_send.at[t], recv_sem=out_recv.at[me], device_id=ids(t), device_id_type=MESH)

    def out_here():
        return pltpu.make_async_copy(
            o_v.at[pl.ds(pl.multiple_of(me * out_rows, out_rows), out_rows)], out_ref.at[:, column(me)], here_sem)

    @pl.when(home)
    def _():
        a = jnp.where(y == 1, 0, 1)
        b = jnp.where(y == 2, 0, 2)

        def start_along(yy):
            for up in (True, False):
                first_hop(yy, up, begin, sends(up))

        def handed(up):
            hand(0, up).wait_recv()

        def near_arrived(yy):
            remote(raw.at[0], block(REACH, yy), near_send.at[0], near_recv.at[REACH, yy], base).wait_recv()

        def pass_on(yy):
            for up, last in ((True, 1), (False, 2)):
                first_hop(yy, up, arrived, gets(up))
                second(yy, up, begin, gets(up) & sends(up) & (yy != last))

        def pass_rest():
            @pl.when(gets(True))
            def _():
                along(HOMES, 1, True, 0, ROWS - CARRIED).wait_recv()
                handed(True)

            second(HOMES, True, begin, gets(True) & sends(True))
            for up, last in ((True, 1), (False, 2)):
                second(last, up, begin, gets(up) & sends(up))

        def fold_rest(up):
            p = REACH - 1 if up else REACH + 1

            @pl.when(gets(up))
            def _():
                if not up:
                    along(HOMES, 1, up, 0, ROWS - CARRIED).wait_recv()
                    handed(up)
                whole(p, HOMES)

        def fold_along(yy):
            for up in (True, False):
                @pl.when(gets(up))
                def _():
                    whole(REACH - 1 if up else REACH + 1, yy)

        def far(yy, up, tile_lo, tile_hi, row_lo, row_hi):
            second(yy, up, arrived, gets(up, 2))

            @pl.when(gets(up, 2))
            def _():
                fold(0 if up else 4, yy, tile_lo, tile_hi, row_lo, row_hi)

        own(0).wait()
        own(1).wait()
        start_along(y)

        @pl.when(y == 0)
        def _():
            send_near(1)
            near(1).wait_send()
            send_near(2)

        @pl.when(y == 1)
        def _():
            send_near(0)
            send_near(2)

        @pl.when(y == 2)
        def _():
            send_near(1)
            send_near(0)
            relay_in().wait_recv()
            relay_out().start()

        near_arrived(a)
        start_along(a)
        for j in (1, 0, 2):
            @pl.when(y != j)
            def _():
                send_q(j)
        pass_on(y)
        near_arrived(b)
        start_along(b)
        near_arrived(HOMES)
        start_along(HOMES)
        pass_on(a)
        own(2).wait()
        for yy in range(YS):
            @pl.when(y != yy)
            def _():
                remote(qraw.at[0], qv.at[rows_of(yy)], q_send.at[0], q_recv.at[yy], base).wait_recv()
        whole(REACH, y)
        whole(REACH, a)
        whole(REACH, b)
        pass_on(b)
        whole(REACH, HOMES)
        fold_along(y)
        pass_rest()
        fold_along(a)
        fold_along(b)

        def finish(yy):
            rows = pl.ds(yy * ROWS, ROWS)
            o_v[rows, :] = (acc[rows, :] / jnp.sum(total[rows, :], axis=1, keepdims=True)).astype(jnp.bfloat16)

            def put(i, c):
                t = yy * heads + i

                @pl.when(t != me)
                def _():
                    out_copy(t).start()

                @pl.when(t == me)
                def _():
                    out_here().start()
                return c

            lax.fori_loop(0, heads, put, 0)

        far(0, False, 0, 3, ROWS, PLANE)
        far(2, True, 0, 3, 0, 2 * ROWS)
        fold_rest(True)
        far(1, False, 0, 3, 2 * ROWS, PLANE)
        fold_rest(False)
        far(3, True, 0, 3, 0, 3 * ROWS)
        finish(1)
        finish(2)
        far(2, False, 0, 2, 3 * ROWS, PLANE)
        finish(3)
        far(1, True, 1, 3, 0, ROWS)
        finish(0)

    @pl.when(relays)
    def _():
        order = (0, 2, 1)
        for n in range(2):
            stage(1, n).wait()
        relay_in().start()
        send_near(0)
        for n in range(2):
            stage(2, n).wait()
        for up in (True, False):
            @pl.when(sends(up))
            def _():
                for j in order:
                    carry(j, up).start()
        relay_in().wait_send()
        near(2).start()
        near(0).wait_send()
        for j in order:
            send_q(j)
        near(2).wait_send()
        for up in (True, False):
            @pl.when(gets(up))
            def _():
                for j in order:
                    carry(j, up).wait_recv()
                    hand(j, up).start()
        for up in (True, False):
            @pl.when(sends(up))
            def _():
                for j in order:
                    carry(j, up).wait_send()

            @pl.when(gets(up))
            def _():
                for j in order:
                    hand(j, up).wait_send()

    def out_wait(t, c):
        @pl.when(t != me)
        def _():
            pltpu.make_async_remote_copy(
                src_ref=o_v.at[pl.ds(0, out_rows)], dst_ref=out_ref.at[:, column(t)], send_sem=out_send.at[0],
                recv_sem=out_recv.at[t], device_id=ids(t), device_id_type=MESH).wait_recv()
        return c

    lax.fori_loop(0, HOMES * heads, out_wait, 0)

    @pl.when(home)
    def _():
        out_here().wait()

        def out_left(i, c):
            out_copy(lax.rem(me + i, peers)).wait_send()
            return c

        lax.fori_loop(1, peers, out_left, 0)
        for up in (True, False):
            for yy in range(YS):
                first_hop(yy, up, left, sends(up))
                if (yy > 0) if up else (yy < HOMES):
                    second(yy, up, left, gets(up) & sends(up))

        @pl.when(y == 2)
        def _():
            relay_out().wait_send()

    for j in range(HOMES):
        sent = y != j
        direct = sent & (y != HOMES) if j == 1 else sent

        @pl.when(direct & (y != HOMES) & ((y != 0) | (j != 1)))
        def _():
            near(j).wait_send()

        @pl.when(sent)
        def _():
            near_q(j).wait_send()


def shards(queries, keys, values, image_tiles):
    heads = lax.axis_size("head")
    dma = pltpu.SemaphoreType.DMA
    half, whole = jnp.bfloat16, jnp.float32
    vmem = pltpu.VMEM
    return pl.pallas_call(
        functools.partial(kernel, heads),
        out_shape=jax.ShapeDtypeStruct((ROWS // heads, HOMES * heads * HD), half),
        in_specs=[pl.BlockSpec(memory_space=pltpu.HBM)] * 4,
        out_specs=pl.BlockSpec(memory_space=pltpu.HBM),
        scratch_shapes=[
            vmem((WIDE, 2, PLANE, HD), half), vmem((HOMES, 2, ROWS, HD), half), vmem((HOMES, ROWS, HD), half),
            vmem((PLANE, HD), half), vmem((2, ROWS, HD), half), vmem((16, WIDE * PLANE), whole),
            vmem((PLANE, HD), whole), vmem((PLANE, HD), whole), vmem((PLANE, HD), whole), vmem((PLANE, HD), half),
            vmem((2, HOMES, 2, CARRIED, HD), half), pltpu.SMEM(image_tiles.shape, jnp.int32), dma((HOMES, 3)), dma((3,)), dma((HOMES,)), dma((WIDE, YS)), dma((HOMES,)), dma((YS,)),
            dma((2, YS)), dma((2, YS)), dma((2, YS)), dma((2, YS)),
            dma((3,)), dma((2, HOMES)), dma((2, HOMES)), dma((2, HOMES)), dma, dma, dma((YS * heads,)), dma((YS * heads,))],
        compiler_params=pltpu.CompilerParams(
            collective_id=0, has_side_effects=True, vmem_limit_bytes=64 * 2**20),
        name="attend",
    )(image_tiles, queries, keys, values)


def solution(mesh):
    placed = (P("seq", "head"), P("seq", "head"), P("seq", "head"), P())
    return jax.shard_map(
        shards, mesh=mesh, in_specs=placed, out_specs=P(("seq", "head"), None), check_vma=False
    )
```

```python
import functools
import math

import jax
import jax.numpy as jnp
from jax import lax
from jax.experimental import pallas as pl
from jax.experimental.pallas import tpu as pltpu
from jax.sharding import PartitionSpec as P

MESH = pl.DeviceIdType.MESH
HD = 128
YS = 4
ZS = 16
HOMES = 3
ROWS = 384
TILES = ROWS // HD
PLANE = YS * ROWS
PLANE_TILES = PLANE // HD
REACH = 2
CARRIED = 2 * HD
WIDE = 2 * REACH + 1
MASKED = -1e30
LOWEST = -1e20
SCALE = math.log2(math.e) / math.sqrt(HD)


def kernel(heads, tiles_hbm, q_ref, k_ref, v_ref, out_ref, win, raw, qraw, qv, relay, bias, acc, top, total, o_v,
           carried, tiles_ref, stage_sem, own_sem, near_send, near_recv, q_send, q_recv, up_send, up_recv, down_send, down_recv,
           relay_sems, met, carry_send, carry_recv, hand_send, tiles_sem, here_sem, out_send, out_recv):
    seq = lax.axis_index("seq")
    head = lax.axis_index("head")
    y = lax.rem(seq, YS)
    z = lax.div(seq, YS)
    base = z * YS
    above = lax.rem(z + 1, ZS) * YS + y
    below = lax.rem(z + ZS - 1, ZS) * YS + y
    home = y < HOMES
    relays = y == HOMES
    peers = YS * heads
    me = y * heads + head

    def block(p, yy, lo=0, hi=ROWS):
        return win.at[p, :, pl.ds(pl.multiple_of(yy * ROWS + lo, HD), hi - lo)]

    def rows_of(yy):
        return pl.ds(pl.multiple_of(yy * ROWS, ROWS), ROWS)

    def stage(j, n):
        dst = qraw.at[j] if n == 2 else raw.at[j, n]
        return pltpu.make_async_copy((k_ref, v_ref, q_ref)[n].at[:, pl.ds(j * HD, HD)], dst, stage_sem.at[j, n])

    def own(n):
        mine = pl.ds(pl.multiple_of(y * HD, HD), HD)
        dst = qv.at[rows_of(y)] if n == 2 else win.at[REACH, n, rows_of(y)]
        return pltpu.make_async_copy((k_ref, v_ref, q_ref)[n].at[:, mine], dst, own_sem.at[n])

    barrier = pltpu.get_barrier_semaphore()

    for other in (above, below):
        pl.semaphore_signal(barrier, inc=1, device_id={"seq": other}, device_id_type=MESH)
    for i in range(1, YS):
        pl.semaphore_signal(barrier, inc=1, device_id={"seq": base + lax.bitwise_and(y + i, YS - 1)}, device_id_type=MESH)

    def others(act):
        for i in range(1, heads):
            act({"head": lax.rem(head + i, heads)})

    others(lambda to: pl.semaphore_signal(barrier, inc=1, device_id=to, device_id_type=MESH))

    fetch = pltpu.make_async_copy(tiles_hbm, tiles_ref, tiles_sem)
    fetch.start()

    @pl.when(home)
    def _():
        for n in range(3):
            own(n).start()

    for n in range(3):
        for j in range(HOMES):
            @pl.when(y != j)
            def _():
                stage(j, n).start()

    def ids(t):
        return {"seq": base + lax.div(t, heads), "head": lax.rem(t, heads)}

    first = (z - REACH) * PLANE_TILES
    keys_at = first + lax.div(lax.broadcasted_iota(jnp.int32, (1, WIDE * PLANE), 1), HD)
    query_at = z * PLANE_TILES + lax.broadcasted_iota(jnp.int32, (16, 1), 0)
    key_image = jnp.where(keys_at < 0, -1, 0)
    query_image = jnp.zeros((16, 1), jnp.int32)
    end = jnp.int32(0)
    fetch.wait()
    for i in range(tiles_ref.shape[0]):
        end = end + tiles_ref[i]
        key_image = key_image + jnp.where(keys_at >= end, 1, 0)
        query_image = query_image + jnp.where(query_at >= end, 1, 0)
    bias[...] = jnp.where(key_image == query_image, 0.0, MASKED)

    @pl.when(home)
    def _():
        acc[...] = jnp.zeros_like(acc)
        total[...] = jnp.zeros_like(total)
        top[...] = jnp.full_like(top, LOWEST)

    pl.semaphore_wait(barrier, YS + heads)

    def remote(src, dst, send, recv, target):
        return pltpu.make_async_remote_copy(
            src_ref=src, dst_ref=dst, send_sem=send, recv_sem=recv,
            device_id={"seq": target}, device_id_type=MESH)

    def near(j):
        return remote(raw.at[j], block(REACH, y), near_send.at[j], near_recv.at[REACH, y], base + j)

    def near_q(j):
        return remote(qraw.at[j], qv.at[rows_of(y)], q_send.at[j], q_recv.at[y], base + j)

    def along(yy, hop, up, lo=0, hi=ROWS):
        src, dst = ((REACH + 1 - hop, REACH - hop) if up else (REACH - 1 + hop, REACH + hop))
        send, recv = (up_send, up_recv) if up else (down_send, down_recv)
        return remote(block(src, yy, lo, hi), block(dst, yy, lo, hi), send.at[hop - 1, yy], recv.at[hop - 1, yy],
                      above if up else below)

    def relay_in():
        return remote(raw.at[1], relay, relay_sems.at[0], relay_sems.at[1], base + 2)

    def relay_out():
        return remote(relay, block(REACH, HOMES), relay_sems.at[2], near_recv.at[REACH, HOMES], base + 1)

    def carry(j, up):
        n = 0 if up else 1
        return remote(raw.at[j, :, pl.ds(ROWS - CARRIED, CARRIED)], carried.at[n, j], carry_send.at[n, j],
                      carry_recv.at[n, j], above if up else below)

    def hand(j, up):
        n, p = (0, REACH - 1) if up else (1, REACH + 1)
        return remote(carried.at[n, j], block(p, HOMES, ROWS - CARRIED, ROWS), hand_send.at[n, j],
                      near_recv.at[p, HOMES], base + j)

    def sends(up):
        return z < ZS - 1 if up else z > 0

    def gets(up, hop=1):
        return z >= hop if up else z < ZS - hop

    def send_near(j):
        for n in range(2):
            stage(j, n).wait()
        near(j).start()

    def send_q(j):
        stage(j, 2).wait()
        near_q(j).start()

    def second(yy, up, act, where):
        short, first_short = (1, HD) if up else (2, 0)

        @pl.when(where & (yy == short))
        def _():
            act(along(yy, 2, up, first_short, first_short + ROWS - HD))

        @pl.when(where & ((yy > short) if up else (yy < short)))
        def _():
            act(along(yy, 2, up))

    def first_hop(yy, up, act, where):
        @pl.when(where & (yy == HOMES))
        def _():
            act(along(yy, 1, up, 0, ROWS - CARRIED))

        @pl.when(where & (yy != HOMES))
        def _():
            act(along(yy, 1, up))

    begin = lambda copy: copy.start()
    arrived = lambda copy: copy.wait_recv()
    left = lambda copy: copy.wait_send()

    def fold(p, yy, tile_lo, tile_hi, row_lo, row_hi):
        count = tile_hi - tile_lo
        rows = pl.ds(row_lo, row_hi - row_lo)
        at = pl.multiple_of(yy * ROWS + tile_lo * HD, HD)
        keys = win[p, 0, pl.ds(at, count * HD), :]
        vals = win[p, 1, pl.ds(at, count * HD), :]
        lanes = pl.ds(pl.multiple_of(p * PLANE + yy * ROWS + tile_lo * HD, HD), count * HD)
        s = lax.dot_general(qv[rows, :], keys, (((1,), (1,)), ((), ())), preferred_element_type=jnp.float32)
        s = jnp.concatenate(
            [s[i:i + HD] * SCALE + bias[pl.ds((row_lo + i) // HD, 1), lanes] for i in range(0, row_hi - row_lo, HD)],
            axis=0)
        parts = [s[:, i * HD:(i + 1) * HD] for i in range(count)]
        old = top[rows, :]
        new = jnp.maximum(old, jnp.max(functools.reduce(jnp.maximum, parts), axis=1, keepdims=True))
        factor = jnp.exp2(old - new)
        weights = [jnp.exp2(part - new) for part in parts]
        total[rows, :] = total[rows, :] * factor + functools.reduce(jnp.add, weights)
        rounded = jnp.concatenate([w.astype(jnp.bfloat16) for w in weights], axis=1)
        acc[rows, :] = acc[rows, :] * factor + jnp.dot(rounded, vals, preferred_element_type=jnp.float32)
        top[rows, :] = new

    def whole(p, yy):
        fold(p, yy, 0, TILES, 0, PLANE)

    def column(t):
        return pl.ds(pl.multiple_of((lax.rem(t, heads) * HOMES + lax.div(t, heads)) * HD, HD), HD)

    out_rows = ROWS // heads

    def out_copy(t):
        return pltpu.make_async_remote_copy(
            src_ref=o_v.at[pl.ds(pl.multiple_of(t * out_rows, out_rows), out_rows)], dst_ref=out_ref.at[:, column(me)],
            send_sem=out_send.at[t], recv_sem=out_recv.at[me], device_id=ids(t), device_id_type=MESH)

    def out_here():
        return pltpu.make_async_copy(
            o_v.at[pl.ds(pl.multiple_of(me * out_rows, out_rows), out_rows)], out_ref.at[:, column(me)], here_sem)

    def met_all():
        others(lambda to: pl.semaphore_signal(met, inc=1, device_id=to, device_id_type=MESH))

    @pl.when(home)
    def _():
        a = jnp.where(y == 1, 0, 1)
        b = jnp.where(y == 2, 0, 2)

        def start_along(yy):
            for up in (True, False):
                first_hop(yy, up, begin, sends(up))

        def handed(up):
            hand(0, up).wait_recv()

        def near_arrived(yy):
            remote(raw.at[0], block(REACH, yy), near_send.at[0], near_recv.at[REACH, yy], base).wait_recv()

        def pass_on(yy):
            for up, last in ((True, 1), (False, 2)):
                first_hop(yy, up, arrived, gets(up))
                second(yy, up, begin, gets(up) & sends(up) & (yy != last))

        def pass_rest():
            @pl.when(gets(True))
            def _():
                along(HOMES, 1, True, 0, ROWS - CARRIED).wait_recv()
                handed(True)

            second(HOMES, True, begin, gets(True) & sends(True))
            for up, last in ((True, 1), (False, 2)):
                second(last, up, begin, gets(up) & sends(up))

        def fold_rest(up):
            p = REACH - 1 if up else REACH + 1

            @pl.when(gets(up))
            def _():
                if not up:
                    along(HOMES, 1, up, 0, ROWS - CARRIED).wait_recv()
                    handed(up)
                whole(p, HOMES)

        def fold_along(yy):
            for up in (True, False):
                @pl.when(gets(up))
                def _():
                    whole(REACH - 1 if up else REACH + 1, yy)

        def far(yy, up, tile_lo, tile_hi, row_lo, row_hi):
            second(yy, up, arrived, gets(up, 2))

            @pl.when(gets(up, 2))
            def _():
                fold(0 if up else 4, yy, tile_lo, tile_hi, row_lo, row_hi)

        own(0).wait()
        own(1).wait()
        start_along(y)

        @pl.when(y == 0)
        def _():
            send_near(1)
            near(1).wait_send()
            send_near(2)

        @pl.when(y == 1)
        def _():
            send_near(0)
            send_near(2)

        @pl.when(y == 2)
        def _():
            send_near(1)
            send_near(0)
            relay_in().wait_recv()
            relay_out().start()

        met_all()
        near_arrived(a)
        start_along(a)
        for j in (1, 0, 2):
            @pl.when(y != j)
            def _():
                send_q(j)
        pass_on(y)
        near_arrived(b)
        start_along(b)
        near_arrived(HOMES)
        start_along(HOMES)
        pass_on(a)
        own(2).wait()
        for yy in range(YS):
            @pl.when(y != yy)
            def _():
                remote(qraw.at[0], qv.at[rows_of(yy)], q_send.at[0], q_recv.at[yy], base).wait_recv()
        whole(REACH, y)
        whole(REACH, a)
        whole(REACH, b)
        pass_on(b)
        whole(REACH, HOMES)
        fold_along(y)
        pass_rest()
        fold_along(a)
        fold_along(b)

        def finish(yy):
            rows = pl.ds(yy * ROWS, ROWS)
            o_v[rows, :] = (acc[rows, :] / jnp.sum(total[rows, :], axis=1, keepdims=True)).astype(jnp.bfloat16)

            def put(i, c):
                t = yy * heads + lax.rem(head + i, heads)

                @pl.when(t != me)
                def _():
                    out_copy(t).start()

                @pl.when(t == me)
                def _():
                    out_here().start()
                return c

            lax.fori_loop(0, heads, put, 0)

        pl.semaphore_wait(met, heads - 1)
        far(0, False, 0, 3, ROWS, PLANE)
        far(2, True, 0, 3, 0, 2 * ROWS)
        fold_rest(True)
        far(1, False, 0, 3, 2 * ROWS, PLANE)
        fold_rest(False)
        far(3, True, 0, 3, 0, 3 * ROWS)
        finish(1)
        finish(2)
        far(2, False, 0, 2, 3 * ROWS, PLANE)
        finish(3)
        far(1, True, 1, 3, 0, ROWS)
        finish(0)

    @pl.when(relays)
    def _():
        order = (0, 2, 1)
        for n in range(2):
            stage(1, n).wait()
        relay_in().start()
        send_near(0)
        for n in range(2):
            stage(2, n).wait()
        for up in (True, False):
            @pl.when(sends(up))
            def _():
                for j in order:
                    carry(j, up).start()
        met_all()
        relay_in().wait_send()
        near(2).start()
        near(0).wait_send()
        for j in order:
            send_q(j)
        near(2).wait_send()
        pl.semaphore_wait(met, heads - 1)
        for up in (True, False):
            @pl.when(gets(up))
            def _():
                for j in order:
                    carry(j, up).wait_recv()
                    hand(j, up).start()
        for up in (True, False):
            @pl.when(sends(up))
            def _():
                for j in order:
                    carry(j, up).wait_send()

            @pl.when(gets(up))
            def _():
                for j in order:
                    hand(j, up).wait_send()

    def out_wait(t, c):
        @pl.when(t != me)
        def _():
            pltpu.make_async_remote_copy(
                src_ref=o_v.at[pl.ds(0, out_rows)], dst_ref=out_ref.at[:, column(t)], send_sem=out_send.at[0],
                recv_sem=out_recv.at[t], device_id=ids(t), device_id_type=MESH).wait_recv()
        return c

    lax.fori_loop(0, HOMES * heads, out_wait, 0)

    @pl.when(home)
    def _():
        out_here().wait()

        def out_left(i, c):
            out_copy(lax.rem(me + i, peers)).wait_send()
            return c

        lax.fori_loop(1, peers, out_left, 0)
        for up in (True, False):
            for yy in range(YS):
                first_hop(yy, up, left, sends(up))
                if (yy > 0) if up else (yy < HOMES):
                    second(yy, up, left, gets(up) & sends(up))

        @pl.when(y == 2)
        def _():
            relay_out().wait_send()

    for j in range(HOMES):
        sent = y != j
        direct = sent & (y != HOMES) if j == 1 else sent

        @pl.when(direct & (y != HOMES) & ((y != 0) | (j != 1)))
        def _():
            near(j).wait_send()

        @pl.when(sent)
        def _():
            near_q(j).wait_send()


def shards(queries, keys, values, image_tiles):
    heads = lax.axis_size("head")
    dma = pltpu.SemaphoreType.DMA
    half, whole = jnp.bfloat16, jnp.float32
    vmem = pltpu.VMEM
    return pl.pallas_call(
        functools.partial(kernel, heads),
        out_shape=jax.ShapeDtypeStruct((ROWS // heads, HOMES * heads * HD), half),
        in_specs=[pl.BlockSpec(memory_space=pltpu.HBM)] * 4,
        out_specs=pl.BlockSpec(memory_space=vmem),
        scratch_shapes=[
            vmem((WIDE, 2, PLANE, HD), half), vmem((HOMES, 2, ROWS, HD), half), vmem((HOMES, ROWS, HD), half),
            vmem((PLANE, HD), half), vmem((2, ROWS, HD), half), vmem((16, WIDE * PLANE), whole),
            vmem((PLANE, HD), whole), vmem((PLANE, HD), whole), vmem((PLANE, HD), whole), vmem((PLANE, HD), half),
            vmem((2, HOMES, 2, CARRIED, HD), half), pltpu.SMEM(image_tiles.shape, jnp.int32), dma((HOMES, 3)), dma((3,)), dma((HOMES,)), dma((WIDE, YS)), dma((HOMES,)), dma((YS,)),
            dma((2, YS)), dma((2, YS)), dma((2, YS)), dma((2, YS)),
            dma((3,)), pltpu.SemaphoreType.REGULAR, dma((2, HOMES)), dma((2, HOMES)), dma((2, HOMES)), dma, dma, dma((YS * heads,)), dma((YS * heads,))],
        compiler_params=pltpu.CompilerParams(
            collective_id=0, has_side_effects=True, vmem_limit_bytes=40 * 2**20),
        name="attend",
    )(*[pltpu.with_memory_space_constraint(x, pltpu.HBM) for x in (image_tiles, queries, keys, values)])


def solution(mesh):
    placed = (P("seq", "head"), P("seq", "head"), P("seq", "head"), P())
    return jax.shard_map(
        shards, mesh=mesh, in_specs=placed, out_specs=P(("seq", "head"), None), check_vma=False
    )
```

```python
import functools
import math

import jax
import jax.numpy as jnp
from jax import lax
from jax.experimental import pallas as pl
from jax.experimental.pallas import tpu as pltpu
from jax.sharding import PartitionSpec as P

MESH = pl.DeviceIdType.MESH
HD = 128
YS = 4
ZS = 16
HOMES = 3
ROWS = 384
TILES = ROWS // HD
PLANE = YS * ROWS
PLANE_TILES = PLANE // HD
REACH = 2
CARRIED = 2 * HD
WIDE = 2 * REACH + 1
MASKED = -1e30
LOWEST = -1e20
SCALE = math.log2(math.e) / math.sqrt(HD)


def kernel(heads, tiles_hbm, q_ref, k_ref, v_ref, out_ref, win, raw, qraw, qv, relay, bias, acc, top, total, o_v,
           carried, tiles_ref, stage_sem, own_sem, near_send, near_recv, q_send, q_recv, up_send, up_recv, down_send, down_recv,
           relay_sems, met, carry_send, carry_recv, hand_send, tiles_sem, here_sem, out_send, out_recv):
    seq = lax.axis_index("seq")
    head = lax.axis_index("head")
    y = lax.rem(seq, YS)
    z = lax.div(seq, YS)
    base = z * YS
    above = lax.rem(z + 1, ZS) * YS + y
    below = lax.rem(z + ZS - 1, ZS) * YS + y
    home = y < HOMES
    relays = y == HOMES
    peers = YS * heads
    me = y * heads + head

    def block(p, yy, lo=0, hi=ROWS):
        return win.at[p, :, pl.ds(pl.multiple_of(yy * ROWS + lo, HD), hi - lo)]

    def rows_of(yy):
        return pl.ds(pl.multiple_of(yy * ROWS, ROWS), ROWS)

    def stage(j, n):
        dst = qraw.at[j] if n == 2 else raw.at[j, n]
        return pltpu.make_async_copy((k_ref, v_ref, q_ref)[n].at[:, pl.ds(j * HD, HD)], dst, stage_sem.at[j, n])

    def own(n):
        mine = pl.ds(pl.multiple_of(y * HD, HD), HD)
        dst = qv.at[rows_of(y)] if n == 2 else win.at[REACH, n, rows_of(y)]
        return pltpu.make_async_copy((k_ref, v_ref, q_ref)[n].at[:, mine], dst, own_sem.at[n])

    barrier = pltpu.get_barrier_semaphore()

    for other in (above, below):
        pl.semaphore_signal(barrier, inc=1, device_id={"seq": other}, device_id_type=MESH)
    for i in range(1, YS):
        pl.semaphore_signal(barrier, inc=1, device_id={"seq": base + lax.bitwise_and(y + i, YS - 1)}, device_id_type=MESH)

    def others(act):
        for i in range(1, heads):
            act({"head": lax.rem(head + i, heads)})

    others(lambda to: pl.semaphore_signal(barrier, inc=1, device_id=to, device_id_type=MESH))

    fetch = pltpu.make_async_copy(tiles_hbm, tiles_ref, tiles_sem)
    fetch.start()

    @pl.when(home)
    def _():
        for n in range(3):
            own(n).start()

    for n in range(3):
        for j in range(HOMES):
            @pl.when(y != j)
            def _():
                stage(j, n).start()

    def ids(t):
        return {"seq": base + lax.div(t, heads), "head": lax.rem(t, heads)}

    first = (z - REACH) * PLANE_TILES
    keys_at = first + lax.div(lax.broadcasted_iota(jnp.int32, (1, WIDE * PLANE), 1), HD)
    query_at = z * PLANE_TILES + lax.broadcasted_iota(jnp.int32, (16, 1), 0)
    key_image = jnp.where(keys_at < 0, -1, 0)
    query_image = jnp.zeros((16, 1), jnp.int32)
    end = jnp.int32(0)
    fetch.wait()
    for i in range(tiles_ref.shape[0]):
        end = end + tiles_ref[i]
        key_image = key_image + jnp.where(keys_at >= end, 1, 0)
        query_image = query_image + jnp.where(query_at >= end, 1, 0)
    bias[...] = jnp.where(key_image == query_image, 0.0, MASKED)

    @pl.when(home)
    def _():
        acc[...] = jnp.zeros_like(acc)
        total[...] = jnp.zeros_like(total)
        top[...] = jnp.full_like(top, LOWEST)

    pl.semaphore_wait(barrier, YS + heads)

    def remote(src, dst, send, recv, target):
        return pltpu.make_async_remote_copy(
            src_ref=src, dst_ref=dst, send_sem=send, recv_sem=recv,
            device_id={"seq": target}, device_id_type=MESH)

    def near(j):
        return remote(raw.at[j], block(REACH, y), near_send.at[j], near_recv.at[REACH, y], base + j)

    def near_q(j):
        return remote(qraw.at[j], qv.at[rows_of(y)], q_send.at[j], q_recv.at[y], base + j)

    def along(yy, hop, up, lo=0, hi=ROWS):
        src, dst = ((REACH + 1 - hop, REACH - hop) if up else (REACH - 1 + hop, REACH + hop))
        send, recv = (up_send, up_recv) if up else (down_send, down_recv)
        return remote(block(src, yy, lo, hi), block(dst, yy, lo, hi), send.at[hop - 1, yy], recv.at[hop - 1, yy],
                      above if up else below)

    def relay_in():
        return remote(raw.at[1], relay, relay_sems.at[0], relay_sems.at[1], base + 2)

    def relay_out():
        return remote(relay, block(REACH, HOMES), relay_sems.at[2], near_recv.at[REACH, HOMES], base + 1)

    def carry(j, up):
        n = 0 if up else 1
        return remote(raw.at[j, :, pl.ds(ROWS - CARRIED, CARRIED)], carried.at[n, j], carry_send.at[n, j],
                      carry_recv.at[n, j], above if up else below)

    def hand(j, up):
        n, p = (0, REACH - 1) if up else (1, REACH + 1)
        return remote(carried.at[n, j], block(p, HOMES, ROWS - CARRIED, ROWS), hand_send.at[n, j],
                      near_recv.at[p, HOMES], base + j)

    def sends(up):
        return z < ZS - 1 if up else z > 0

    def gets(up, hop=1):
        return z >= hop if up else z < ZS - hop

    def send_near(j):
        for n in range(2):
            stage(j, n).wait()
        near(j).start()

    def send_q(j):
        stage(j, 2).wait()
        near_q(j).start()

    def second(yy, up, act, where):
        short, first_short = (1, HD) if up else (2, 0)

        @pl.when(where & (yy == short))
        def _():
            act(along(yy, 2, up, first_short, first_short + ROWS - HD))

        @pl.when(where & ((yy > short) if up else (yy < short)))
        def _():
            act(along(yy, 2, up))

    def first_hop(yy, up, act, where):
        @pl.when(where & (yy == HOMES))
        def _():
            act(along(yy, 1, up, 0, ROWS - CARRIED))

        @pl.when(where & (yy != HOMES))
        def _():
            act(along(yy, 1, up))

    begin = lambda copy: copy.start()
    arrived = lambda copy: copy.wait_recv()
    left = lambda copy: copy.wait_send()

    def fold(p, yy, tile_lo, tile_hi, row_lo, row_hi):
        count = tile_hi - tile_lo
        rows = pl.ds(row_lo, row_hi - row_lo)
        at = pl.multiple_of(yy * ROWS + tile_lo * HD, HD)
        keys = win[p, 0, pl.ds(at, count * HD), :]
        vals = win[p, 1, pl.ds(at, count * HD), :]
        lanes = pl.ds(pl.multiple_of(p * PLANE + yy * ROWS + tile_lo * HD, HD), count * HD)
        s = lax.dot_general(qv[rows, :], keys, (((1,), (1,)), ((), ())), preferred_element_type=jnp.float32)
        s = jnp.concatenate(
            [s[i:i + HD] * SCALE + bias[pl.ds((row_lo + i) // HD, 1), lanes] for i in range(0, row_hi - row_lo, HD)],
            axis=0)
        parts = [s[:, i * HD:(i + 1) * HD] for i in range(count)]
        old = top[rows, :]
        new = jnp.maximum(old, jnp.max(functools.reduce(jnp.maximum, parts), axis=1, keepdims=True))
        factor = jnp.exp2(old - new)
        weights = [jnp.exp2(part - new) for part in parts]
        total[rows, :] = total[rows, :] * factor + functools.reduce(jnp.add, weights)
        rounded = jnp.concatenate([w.astype(jnp.bfloat16) for w in weights], axis=1)
        acc[rows, :] = acc[rows, :] * factor + jnp.dot(rounded, vals, preferred_element_type=jnp.float32)
        top[rows, :] = new

    def whole(p, yy):
        fold(p, yy, 0, TILES, 0, PLANE)

    def column(t):
        return pl.ds(pl.multiple_of((lax.rem(t, heads) * HOMES + lax.div(t, heads)) * HD, HD), HD)

    out_rows = ROWS // heads

    def out_copy(t):
        return pltpu.make_async_remote_copy(
            src_ref=o_v.at[pl.ds(pl.multiple_of(t * out_rows, out_rows), out_rows)], dst_ref=out_ref.at[:, column(me)],
            send_sem=out_send.at[t], recv_sem=out_recv.at[me], device_id=ids(t), device_id_type=MESH)

    def out_here():
        return pltpu.make_async_copy(
            o_v.at[pl.ds(pl.multiple_of(me * out_rows, out_rows), out_rows)], out_ref.at[:, column(me)], here_sem)

    def met_all():
        others(lambda to: pl.semaphore_signal(met, inc=1, device_id=to, device_id_type=MESH))

    @pl.when(home)
    def _():
        a = jnp.where(y == 1, 0, 1)
        b = jnp.where(y == 2, 0, 2)

        def start_along(yy):
            for up in (True, False):
                first_hop(yy, up, begin, sends(up))

        def handed(up):
            hand(0, up).wait_recv()

        def near_arrived(yy):
            remote(raw.at[0], block(REACH, yy), near_send.at[0], near_recv.at[REACH, yy], base).wait_recv()

        def pass_on(yy):
            for up, last in ((True, 1), (False, 2)):
                first_hop(yy, up, arrived, gets(up))
                second(yy, up, begin, gets(up) & sends(up) & (yy != last))

        def pass_rest():
            @pl.when(gets(True))
            def _():
                along(HOMES, 1, True, 0, ROWS - CARRIED).wait_recv()
                handed(True)

            second(HOMES, True, begin, gets(True) & sends(True))
            for up, last in ((True, 1), (False, 2)):
                second(last, up, begin, gets(up) & sends(up))

        def fold_rest(up):
            p = REACH - 1 if up else REACH + 1

            @pl.when(gets(up))
            def _():
                if not up:
                    along(HOMES, 1, up, 0, ROWS - CARRIED).wait_recv()
                    handed(up)
                whole(p, HOMES)

        def fold_along(yy):
            for up in (True, False):
                @pl.when(gets(up))
                def _():
                    whole(REACH - 1 if up else REACH + 1, yy)

        def far(yy, up, tile_lo, tile_hi, row_lo, row_hi):
            second(yy, up, arrived, gets(up, 2))

            @pl.when(gets(up, 2))
            def _():
                fold(0 if up else 4, yy, tile_lo, tile_hi, row_lo, row_hi)

        own(0).wait()
        own(1).wait()
        start_along(y)

        @pl.when(y == 0)
        def _():
            send_near(1)
            near(1).wait_send()
            send_near(2)

        @pl.when(y == 1)
        def _():
            send_near(0)
            send_near(2)

        @pl.when(y == 2)
        def _():
            send_near(1)
            send_near(0)
            relay_in().wait_recv()
            relay_out().start()

        met_all()
        near_arrived(a)
        start_along(a)
        for j in (1, 0, 2):
            @pl.when(y != j)
            def _():
                send_q(j)
        pass_on(y)
        near_arrived(b)
        start_along(b)
        near_arrived(HOMES)
        start_along(HOMES)
        pass_on(a)
        own(2).wait()
        for yy in range(YS):
            @pl.when(y != yy)
            def _():
                remote(qraw.at[0], qv.at[rows_of(yy)], q_send.at[0], q_recv.at[yy], base).wait_recv()
        whole(REACH, y)
        whole(REACH, a)
        whole(REACH, b)
        pass_on(b)
        whole(REACH, HOMES)
        fold_along(y)
        pass_rest()
        fold_along(a)
        fold_along(b)

        def finish(yy):
            rows = pl.ds(yy * ROWS, ROWS)
            o_v[rows, :] = (acc[rows, :] / jnp.sum(total[rows, :], axis=1, keepdims=True)).astype(jnp.bfloat16)

            def put(i, c):
                t = yy * heads + lax.rem(head + i, heads)

                @pl.when(t != me)
                def _():
                    out_copy(t).start()

                @pl.when(t == me)
                def _():
                    out_here().start()
                return c

            lax.fori_loop(0, heads, put, 0)

        pl.semaphore_wait(met, heads - 1)
        far(0, False, 0, 3, ROWS, PLANE)
        far(2, True, 0, 3, 0, 2 * ROWS)
        fold_rest(True)
        far(1, False, 0, 3, 2 * ROWS, PLANE)
        fold_rest(False)
        far(3, True, 0, 3, 0, 3 * ROWS)
        far(1, True, 1, 3, 0, ROWS)
        finish(0)
        finish(2)
        far(2, False, 0, 2, 3 * ROWS, PLANE)
        finish(3)
        finish(1)

    @pl.when(relays)
    def _():
        order = (0, 2, 1)
        for n in range(2):
            stage(1, n).wait()
        relay_in().start()
        send_near(0)
        for n in range(2):
            stage(2, n).wait()
        for up in (True, False):
            @pl.when(sends(up))
            def _():
                for j in order:
                    carry(j, up).start()
        met_all()
        relay_in().wait_send()
        near(2).start()
        near(0).wait_send()
        for j in order:
            send_q(j)
        near(2).wait_send()
        pl.semaphore_wait(met, heads - 1)
        for up in (True, False):
            @pl.when(gets(up))
            def _():
                for j in order:
                    carry(j, up).wait_recv()
                    hand(j, up).start()
        for up in (True, False):
            @pl.when(sends(up))
            def _():
                for j in order:
                    carry(j, up).wait_send()

            @pl.when(gets(up))
            def _():
                for j in order:
                    hand(j, up).wait_send()

    def out_wait(t, c):
        @pl.when(t != me)
        def _():
            pltpu.make_async_remote_copy(
                src_ref=o_v.at[pl.ds(0, out_rows)], dst_ref=out_ref.at[:, column(t)], send_sem=out_send.at[0],
                recv_sem=out_recv.at[t], device_id=ids(t), device_id_type=MESH).wait_recv()
        return c

    lax.fori_loop(0, HOMES * heads, out_wait, 0)

    @pl.when(home)
    def _():
        out_here().wait()

        def out_left(i, c):
            out_copy(lax.rem(me + i, peers)).wait_send()
            return c

        lax.fori_loop(1, peers, out_left, 0)
        for up in (True, False):
            for yy in range(YS):
                first_hop(yy, up, left, sends(up))
                if (yy > 0) if up else (yy < HOMES):
                    second(yy, up, left, gets(up) & sends(up))

        @pl.when(y == 2)
        def _():
            relay_out().wait_send()

    for j in range(HOMES):
        sent = y != j
        direct = sent & (y != HOMES) if j == 1 else sent

        @pl.when(direct & (y != HOMES) & ((y != 0) | (j != 1)))
        def _():
            near(j).wait_send()

        @pl.when(sent)
        def _():
            near_q(j).wait_send()


def shards(queries, keys, values, image_tiles):
    heads = lax.axis_size("head")
    dma = pltpu.SemaphoreType.DMA
    half, whole = jnp.bfloat16, jnp.float32
    vmem = pltpu.VMEM
    return pl.pallas_call(
        functools.partial(kernel, heads),
        out_shape=jax.ShapeDtypeStruct((ROWS // heads, HOMES * heads * HD), half),
        in_specs=[pl.BlockSpec(memory_space=pltpu.HBM)] * 4,
        out_specs=pl.BlockSpec(memory_space=vmem),
        scratch_shapes=[
            vmem((WIDE, 2, PLANE, HD), half), vmem((HOMES, 2, ROWS, HD), half), vmem((HOMES, ROWS, HD), half),
            vmem((PLANE, HD), half), vmem((2, ROWS, HD), half), vmem((16, WIDE * PLANE), whole),
            vmem((PLANE, HD), whole), vmem((PLANE, HD), whole), vmem((PLANE, HD), whole), vmem((PLANE, HD), half),
            vmem((2, HOMES, 2, CARRIED, HD), half), pltpu.SMEM(image_tiles.shape, jnp.int32), dma((HOMES, 3)), dma((3,)), dma((HOMES,)), dma((WIDE, YS)), dma((HOMES,)), dma((YS,)),
            dma((2, YS)), dma((2, YS)), dma((2, YS)), dma((2, YS)),
            dma((3,)), pltpu.SemaphoreType.REGULAR, dma((2, HOMES)), dma((2, HOMES)), dma((2, HOMES)), dma, dma, dma((YS * heads,)), dma((YS * heads,))],
        compiler_params=pltpu.CompilerParams(
            collective_id=0, has_side_effects=True, vmem_limit_bytes=40 * 2**20),
        name="attend",
    )(*[pltpu.with_memory_space_constraint(x, pltpu.HBM) for x in (image_tiles, queries, keys, values)])


def solution(mesh):
    placed = (P("seq", "head"), P("seq", "head"), P("seq", "head"), P())
    return jax.shard_map(
        shards, mesh=mesh, in_specs=placed, out_specs=P(("seq", "head"), None), check_vma=False
    )
```
